32 devices in a mesh: rep: 1, seq: 8 (over z, y), head: 2 (over x), sub: 2 (over core).
Axes of the slice: x: 2, y: 2, z: 4, core: 2. Of those that a mesh axis runs over, the one named last changes fastest.
Arguments:
- head_query_rows: bfloat16 [2048, 2048], P(('rep', 'seq', 'sub'), 'head'), may hold values from -6 to 6, as said below
- head_key_rows: bfloat16 [2048, 2048], P(('rep', 'seq', 'sub'), 'head'), may hold values from -6 to 6, as said below
- head_value_rows: bfloat16 [2048, 2048], P(('rep', 'seq', 'sub'), 'head'), may hold values from -6 to 6
- output_gradient: bfloat16 [2048, 4096], P(('rep', 'seq', 'sub'), 'head'), may hold values from -6 to 6
- output_matrix: bfloat16 [2048, 4096], P('head', 'sub'), may hold values from -0.125 to 0.125
- adapter_down_weight: bfloat16 [2048, 16], P('head'), may hold values from -0.125 to 0.125
- adapter_up_weight: bfloat16 [16, 4096], replicated, may hold values from -0.09375 to 0.09375
Outputs:
- query_gradient: bfloat16 [2048, 2048], P(('rep', 'seq', 'sub'), 'head')
- key_gradient: bfloat16 [2048, 2048], P(('rep', 'seq', 'sub'), 'head')
- value_gradient: bfloat16 [2048, 2048], P(('rep', 'seq', 'sub'), 'head')
- adapter_down_gradient: float32 [2048, 16], P(('rep', 'head'))
- adapter_up_gradient: float32 [16, 4096], P('rep', 'head')
The draws below stay inside these ranges and needn't reach their ends.
Inputs may be any that keep to these rules, and one draw needn't show every extreme that they name: `head_query_rows`: entries of the queries are real values within the range. `head_key_rows`: entries of the keys are real values within the range.
All inputs are finite; a program needn't handle non-finite values.
Results may differ from the reference program's by a relative error of at most 0.029.
Values may be sent and summed in bfloat16 or wider, within the bound.
A program may use at most 64 MiB of HBM per device.

```python
import jax
import jax.numpy as jnp
from jax import lax

HD = 128
HEADS = 16
MODEL_WIDTH = 4096
LOW_RANK = 16
GROUP = 2048
TOK_DEV = 128
SEQ = 2048
HEAD_FEATURES = 2048


def paired_rows(key):
    base = jax.random.fold_in(key, 11)
    streams = jax.random.split(base, 2)
    shape = (SEQ, HEAD_FEATURES)
    query_raw = jnp.clip(jax.random.normal(streams[0], shape, jnp.float32), -6.0, 6.0)
    key_raw = jnp.clip(jax.random.normal(streams[1], shape, jnp.float32), -6.0, 6.0)
    return (query_raw, key_raw)


def draw_head_query_rows(key, part):
    return paired_rows(key)[0].astype(jnp.bfloat16)


def draw_head_key_rows(key, part):
    return paired_rows(key)[1].astype(jnp.bfloat16)


def level_of(stream_key, extent, cuts, least, largest):
    gain, own = 1.0, jax.random.fold_in(stream_key, 6)
    for dim, blocks in cuts:
        steps = jnp.exp(jax.random.uniform(jax.random.fold_in(own, dim), (blocks,), jnp.float32, least / len(cuts), largest / len(cuts)))
        gain = gain * jnp.repeat(steps, extent[dim] // blocks).reshape([-1 if axis == dim else 1 for axis in range(len(extent))])
    return gain


def noise(rng, extent, spread, limit, cuts=(), held_as=jnp.bfloat16):
    entries = jax.random.normal(rng, extent, jnp.float32) * spread
    if len(cuts) > 0:
        entries = level_of(rng, extent, cuts, -0.22, 0.18) * entries
    return jnp.clip(entries, min=-limit, max=limit).astype(held_as)


def setup_inputs(seed: int = 0, part: int = 0) -> dict:
    streams_of = jax.random.split(jax.random.key(seed), 8)
    part_splits = jax.random.split(jax.random.fold_in(streams_of[7], part), 8)
    return {
        "head_query_rows": draw_head_query_rows(jax.random.fold_in(jax.random.fold_in(streams_of[7], part), 71), part),
        "head_key_rows": draw_head_key_rows(jax.random.fold_in(jax.random.fold_in(streams_of[7], part), 71), part),
        "head_value_rows": noise(part_splits[2], (SEQ, HEAD_FEATURES), 1.0, 6.0, ((0, 16), (1, 2))),
        "output_gradient": noise(part_splits[3], (SEQ, MODEL_WIDTH), 1.0, 6.0, ((0, 16), (1, 2))),
        "output_matrix": noise(streams_of[4], (HEAD_FEATURES, MODEL_WIDTH), HEAD_FEATURES ** -0.5, 0.125, ((0, 2), (1, 2))),
        "adapter_down_weight": noise(streams_of[5], (HEAD_FEATURES, LOW_RANK), HEAD_FEATURES ** -0.5, 0.125, ((0, 2),)),
        "adapter_up_weight": noise(streams_of[6], (LOW_RANK, MODEL_WIDTH), MODEL_WIDTH ** -0.5, 0.09375),
    }


def exact_dot(left, right):
    return jnp.dot(left.astype(jnp.float32), right.astype(jnp.float32), precision=lax.Precision.HIGHEST)


def group_pass(pieces):
    query_g, key_g, value_g, dout_g = pieces
    inverse = HD ** -0.5
    row_idx = lax.broadcasted_iota(jnp.int32, (GROUP, GROUP), 0)
    col_idx = lax.broadcasted_iota(jnp.int32, (GROUP, GROUP), 1)
    visible = col_idx <= row_idx
    scores = exact_dot(query_g, key_g.T) * inverse
    scores = jnp.where(visible, scores, -jnp.inf)
    highest = jnp.max(scores, axis=1, keepdims=True)
    powers = jnp.exp(scores - highest)
    prob = powers / jnp.sum(powers, axis=1, keepdims=True)
    prob_lo = prob.astype(jnp.bfloat16)
    attn_g = exact_dot(prob_lo, value_g).astype(jnp.bfloat16)
    dprob = exact_dot(dout_g, value_g.T)
    delta = jnp.sum(prob * dprob, axis=1, keepdims=True)
    dscore = (prob * (dprob - delta) * inverse).astype(jnp.bfloat16)
    grad_q = exact_dot(dscore, key_g).astype(jnp.bfloat16)
    blocks = GROUP // TOK_DEV
    score_grad_blocks = dscore.reshape(blocks, TOK_DEV, GROUP).astype(jnp.float32)
    query_tiles = query_g.reshape(blocks, TOK_DEV, HD).astype(jnp.float32)
    key_partials = jnp.einsum("srz,srj->szj", score_grad_blocks, query_tiles, precision=lax.Precision.HIGHEST)
    key_partials = lax.optimization_barrier(key_partials.astype(jnp.bfloat16)).astype(jnp.float32)
    grad_k = jnp.sum(key_partials, axis=0).astype(jnp.bfloat16)
    probability_blocks = prob_lo.reshape(blocks, TOK_DEV, GROUP).astype(jnp.float32)
    output_grad_blocks = dout_g.reshape(blocks, TOK_DEV, HD).astype(jnp.float32)
    value_partials = jnp.einsum("srz,srj->szj", probability_blocks, output_grad_blocks, precision=lax.Precision.HIGHEST)
    value_partials = lax.optimization_barrier(value_partials.astype(jnp.bfloat16)).astype(jnp.float32)
    grad_v = jnp.sum(value_partials, axis=0).astype(jnp.bfloat16)
    return attn_g, grad_q, grad_k, grad_v


def heads_pass(query_h, key_h, value_h, dout_h, roll_by):
    count = query_h.shape[0]

    def prepare(tensor):
        return jnp.roll(tensor, -roll_by, axis=1).reshape(count * (SEQ // GROUP), GROUP, HD)

    results = lax.map(group_pass, (prepare(query_h), prepare(key_h), prepare(value_h), prepare(dout_h)))

    def restore(tensor):
        return jnp.roll(tensor.reshape(count, SEQ, HD), roll_by, axis=1)

    return tuple(restore(result) for result in results)


def split_heads(tensor):
    return tensor.reshape(SEQ, HEADS, HD).transpose(1, 0, 2)


def join_heads(tensor):
    return tensor.transpose(1, 0, 2).reshape(SEQ, HEAD_FEATURES)


def reference(head_query_rows, head_key_rows, head_value_rows, output_gradient, output_matrix, adapter_down_weight, adapter_up_weight):
    adapter_upward = exact_dot(output_gradient, adapter_up_weight.T)
    projected_output = exact_dot(output_gradient, output_matrix.T)
    adapter_backward = exact_dot(adapter_upward, adapter_down_weight.T)
    attention_gradient = (projected_output + 2.0 * adapter_backward).astype(jnp.bfloat16)
    per_head = [split_heads(tensor) for tensor in (head_query_rows, head_key_rows, head_value_rows, attention_gradient)]
    half_heads = HEADS // 2
    plain_heads = heads_pass(*[tensor[:half_heads] for tensor in per_head], 0)
    moved_heads = heads_pass(*[tensor[half_heads:] for tensor in per_head], GROUP // 2)
    joined = [join_heads(jnp.concatenate((first, second), axis=0)) for first, second in zip(plain_heads, moved_heads)]
    attention_output, query_gradient, key_gradient, value_gradient = joined
    adapter_middle = exact_dot(attention_output, adapter_down_weight)
    adapter_down_gradient = 2.0 * exact_dot(attention_output.T, adapter_upward)
    adapter_up_gradient = 2.0 * exact_dot(adapter_middle.T, output_gradient)
    return query_gradient, key_gradient, value_gradient, adapter_down_gradient, adapter_up_gradient
```

```python
import jax
import jax.numpy as jnp
from jax import lax
from jax.experimental import pallas as pl
from jax.experimental.pallas import tpu as pltpu
from jax.sharding import PartitionSpec as P

HD = 128
GROUP = 2048


def passed_along(value, axis, by):
    peers = lax.axis_size(axis)
    return lax.ppermute(value, axis, [(i, (i + by) % peers) for i in range(peers)])


def placed_visible(row_count, window_rows, seq_total, first_row, back_rows, roll_by):
    query_pos = first_row + lax.broadcasted_iota(jnp.int32, (row_count, window_rows), 0)
    key_pos = (
        first_row
        - back_rows
        + seq_total
        + lax.broadcasted_iota(jnp.int32, (row_count, window_rows), 1)
    ) % seq_total
    query_order = (query_pos - roll_by + seq_total) % seq_total
    key_order = (key_pos - roll_by + seq_total) % seq_total
    return (query_order // GROUP == key_order // GROUP) & (key_order <= query_order)


def softmax_rows(query_head, keys_head, visible):
    scores = lax.dot_general(
        query_head, keys_head, (((1,), (1,)), ((), ())), preferred_element_type=jnp.float32
    )
    scores = jnp.where(visible, scores * HD ** (-0.5), -jnp.inf)
    highest = jnp.max(scores, axis=1, keepdims=True)
    powers = jnp.exp(scores - highest)
    return powers / jnp.sum(powers, axis=1, keepdims=True)


def head_forward(query_head, window_head, visible):
    prob = softmax_rows(query_head, window_head[0], visible)
    return jnp.dot(
        prob.astype(jnp.bfloat16), window_head[1], preferred_element_type=jnp.float32
    ).astype(jnp.bfloat16)


def head_backward(query_head, window_head, dout_head, visible):
    prob = softmax_rows(query_head, window_head[0], visible)
    prob_lo = prob.astype(jnp.bfloat16)
    dprob = lax.dot_general(
        dout_head, window_head[1], (((1,), (1,)), ((), ())), preferred_element_type=jnp.float32
    )
    delta = jnp.sum(prob * dprob, axis=1, keepdims=True)
    dscore = (prob * (dprob - delta) * HD ** (-0.5)).astype(jnp.bfloat16)
    grad_q = jnp.dot(dscore, window_head[0], preferred_element_type=jnp.float32).astype(
        jnp.bfloat16
    )
    grad_k = lax.dot_general(
        dscore, query_head, (((0,), (0,)), ((), ())), preferred_element_type=jnp.float32
    )
    grad_v = lax.dot_general(
        prob_lo, dout_head, (((0,), (0,)), ((), ())), preferred_element_type=jnp.float32
    )
    return (grad_q, jnp.stack((grad_k.astype(jnp.bfloat16), grad_v.astype(jnp.bfloat16))))


def attend_window(query_rows, window, dout_rows, visible):
    row_count, feat_count = query_rows.shape
    heads_here = feat_count // HD
    window_rows = window.shape[1]
    window_heads = window.reshape(2, window_rows, heads_here, HD).transpose(2, 0, 1, 3)
    query_heads = query_rows.reshape(row_count, heads_here, HD).transpose(1, 0, 2)
    dout_heads = dout_rows.reshape(row_count, heads_here, HD).transpose(1, 0, 2)
    attn_heads = lax.map(
        lambda pieces: head_forward(pieces[0], pieces[1], visible), (query_heads, window_heads)
    )
    grad_q_heads, pair_heads = lax.map(
        lambda pieces: head_backward(pieces[0], pieces[1], pieces[2], visible),
        (query_heads, window_heads, dout_heads),
    )
    attention_output = attn_heads.transpose(1, 0, 2).reshape(row_count, feat_count)
    query_gradient = grad_q_heads.transpose(1, 0, 2).reshape(row_count, feat_count)
    pair_grads = pair_heads.transpose(1, 2, 0, 3).reshape(2, window_rows, feat_count)
    return (attention_output, query_gradient, pair_grads)


def on_device_windows(
    head_query_rows,
    head_key_rows,
    head_value_rows,
    output_gradient,
    output_matrix,
    adapter_down_weight,
    adapter_up_weight,
):
    tokens_dev, feat_dev = head_query_rows.shape
    head_index = lax.axis_index("head")
    shifted = head_index >= lax.axis_size("head") // 2
    total_gradient = lax.all_gather(output_gradient, "head", axis=1, tiled=True)
    projected_output = lax.dot_general(
        total_gradient,
        lax.all_gather(output_matrix, "sub", axis=1, tiled=True),
        (((1,), (1,)), ((), ())),
        preferred_element_type=jnp.float32,
    )
    adapter_upward = lax.dot_general(
        total_gradient,
        adapter_up_weight,
        (((1,), (1,)), ((), ())),
        preferred_element_type=jnp.float32,
    )
    adapter_backward = jnp.dot(
        adapter_upward, adapter_down_weight.astype(jnp.float32).T, precision=lax.Precision.HIGHEST
    )
    attention_gradient = (projected_output + 2.0 * adapter_backward).astype(jnp.bfloat16)
    sub_count = lax.axis_size("sub")
    block_rows = tokens_dev * sub_count
    seq_total = block_rows * lax.axis_size("seq")
    reach = max(GROUP // block_rows - 1, 1)
    roll_by = jnp.where(shifted, GROUP // 2, 0)
    stacked = jnp.stack((head_query_rows, head_key_rows, head_value_rows, attention_gradient))
    moved = lax.all_to_all(stacked, "sub", split_axis=2, concat_axis=1, tiled=True)
    own_pair = moved[1:3]
    received = [passed_along(own_pair, "seq", distance) for distance in range(reach, 0, -1)]
    window = jnp.concatenate(received + [own_pair], axis=1)
    first_row = lax.axis_index("seq") * block_rows
    visible = placed_visible(
        block_rows, window.shape[1], seq_total, first_row, reach * block_rows, roll_by
    )
    attn_local, grad_q_local, pair_grads = attend_window(moved[0], window, moved[3], visible)
    running = pair_grads[:, reach * block_rows :].astype(jnp.float32)
    for distance in range(1, reach + 1):
        begin_row = (reach - distance) * block_rows
        block_terms = pair_grads[:, begin_row : begin_row + block_rows]
        returned = passed_along(block_terms, "seq", -distance)
        running = running + returned.astype(jnp.float32)
    pair_local = running.astype(jnp.bfloat16)
    back = jnp.stack((attn_local, grad_q_local, pair_local[0], pair_local[1]))
    restored = lax.all_to_all(back, "sub", split_axis=1, concat_axis=2, tiled=True)
    attention_output = restored[0]
    query_gradient = restored[1]
    key_gradient = restored[2]
    value_gradient = restored[3]
    middle_piece = jnp.dot(
        attention_output, adapter_down_weight, preferred_element_type=jnp.float32
    )
    down_gradient_part = 2.0 * jnp.dot(
        attention_output.astype(jnp.float32).T, adapter_upward, precision=lax.Precision.HIGHEST
    )
    adapter_middle = lax.psum(middle_piece, "head")
    up_gradient_part = 2.0 * jnp.dot(
        adapter_middle.T, output_gradient.astype(jnp.float32), precision=lax.Precision.HIGHEST
    )
    adapter_down_gradient, adapter_up_gradient = lax.psum(
        (down_gradient_part, up_gradient_part), ("seq", "sub")
    )
    return (
        query_gradient,
        key_gradient,
        value_gradient,
        adapter_down_gradient,
        adapter_up_gradient,
    )


SCALE = HD ** (-0.5)
F32, BF16 = jnp.float32, jnp.bfloat16


def dot_nn(left, right):
    return lax.dot_general(left, right, (((1,), (0,)), ((), ())), preferred_element_type=F32)


def dot_nt(left, right):
    return lax.dot_general(left, right, (((1,), (1,)), ((), ())), preferred_element_type=F32)


MESH = pl.DeviceIdType.MESH
BLOCKS = 4
LOG2E = 1.4426950408889634
NONE = -1e30


class Slots:
    def __init__(self):
        self.count = 0

    def take(self, many=1):
        first = self.count
        self.count += many
        return first


def make_slots():
    names = dict(
        k=4, q=4, v=4, g=4, kx=4, vx=4, qx=4, gx=4, kp=4, vp=4, kxp=4, vxp=4, big=2, w=1, gl=1,
        part=1, lora=1, up=8, stat=1, theirs=6, hq=8, hk=8, hv=8, rq=4, rk=4, rv=4,
        mid=8, midx=1, us=1, ur=8, ug=8, uh=1, ds=1, dn=8,
    )
    slots, places = Slots(), {}
    for name, many in names.items():
        places[name] = slots.take(many)
    return places, slots.count


PLACES, RECEIVES = make_slots()
SENDS = 160


def combine(mine, other):
    top = jnp.maximum(mine[0], other[0])
    c = SCALE * LOG2E
    e1, e2 = jnp.exp2((mine[0] - top) * c), jnp.exp2((other[0] - top) * c)
    w = 1.0 / (mine[1] * e1 + other[1] * e2)
    w1, w2 = e1 * w, e2 * w
    return w1, w1 * mine[2] + w2 * other[2]


def fused_kernel(
    q_ref, k_ref, v_ref, g_ref, w_ref, a_ref, b_ref,
    dq_out, dk_out, dv_out, down_out, up_out,
    qb, kb, vb, gb, qr, kr, vr, gr,
    big, wb, gl, xb, xs, xr, ls, lr, lub, dob,
    kt, vt, probs, ot, gt, acc, stat_s, stat_r, ts, tr, hs, dqs,
    rk, rv, rq, ms, mb, mxs, mxr, us, usr, urr, uf, dss, dsr, dnr,
    ssem, rsem,
):
    s, x, c = lax.axis_index("seq"), lax.axis_index("head"), lax.axis_index("sub")
    n = BLOCKS
    half, j = s // n, lax.rem(s, n)
    late = lax.rem(half + x, 2) == 1
    early = lax.rem(half + x, 2) == 0
    partner = {"sub": 1 - c}
    sends = []
    counter = Slots()

    def at(base, many):
        return pl.ds(pl.multiple_of(base, many), many)

    def send(src, dst, place, to, when=None):
        copy = pltpu.make_async_remote_copy(
            src_ref=src, dst_ref=dst, send_sem=ssem.at[counter.take()], recv_sem=rsem.at[place],
            device_id=to, device_id_type=MESH,
        )
        if when is None:
            copy.start()
        else:
            pl.when(when)(copy.start)
        sends.append((copy, when))

    def got(dst, place):
        pltpu.make_async_remote_copy(
            src_ref=dst, dst_ref=dst, send_sem=ssem.at[0], recv_sem=rsem.at[place],
            device_id=partner, device_id_type=MESH,
        ).wait_recv()

    def local(src, dst, place):
        copy = pltpu.make_async_copy(src, dst, rsem.at[place])
        copy.start()
        return copy

    def near(d):
        o = lax.rem(j + d, n)
        return o, {"seq": half * n + o}

    def far(d):
        o = lax.rem(j + d, n)
        return o, {"seq": (1 - half) * n + o}

    p = PLACES
    barrier = pltpu.get_barrier_semaphore()
    greeted = [near(d)[1] for d in range(1, n)] + [far(d)[1] for d in range(n)]
    greeted += [partner, {"head": 1 - x}, {"head": 1 - x, "sub": 1 - c}]
    for device in greeted:
        pl.semaphore_signal(barrier, inc=1, device_id=device, device_id_type=MESH)
    pl.semaphore_wait(barrier, len(greeted))

    rows = at(c * HD, HD)
    send(g_ref, big.at[rows], p["big"] + c, {"head": 1 - x, "sub": x})
    send(g_ref, big.at[rows], p["big"] + c, partner, when=c != x)

    @pl.when(c == x)
    def _():
        local(g_ref, big.at[rows], p["big"] + c)

    w_copy = local(w_ref, wb, p["w"])
    mine_k, mine_q = at(j * 2 * HD + c * HD, HD), at(j * HD, HD)
    for d in range(1, n):
        o, to = near(d)
        cols = at(o * 2 * HD, 2 * HD)
        send(k_ref.at[:, cols], kb.at[mine_k], p["k"] + j, to)
        send(q_ref.at[:, cols], qb.at[mine_q], p["q"] + j, to)
    for d in range(n):
        o, to = far(d)
        first, second = at(o * 2 * HD, HD), at(o * 2 * HD + HD, HD)
        send(k_ref.at[:, first], kr.at[mine_k], p["kx"] + j, to, when=early)
        send(q_ref.at[:, second], qr.at[mine_q], p["qx"] + j, to, when=late)
    for d in range(1, n):
        o, to = near(d)
        send(v_ref.at[:, at(o * 2 * HD, 2 * HD)], vb.at[mine_k], p["v"] + j, to)
    for d in range(n):
        o, to = far(d)
        send(v_ref.at[:, at(o * 2 * HD, HD)], vr.at[mine_k], p["vx"] + j, to, when=early)
    own = at(j * 2 * HD, 2 * HD)
    own_copies = [
        local(k_ref.at[:, own], kb.at[mine_k], p["k"] + j),
        local(v_ref.at[:, own], vb.at[mine_k], p["v"] + j),
        local(q_ref.at[:, own], qb.at[mine_q], p["q"] + j),
    ]
    send(k_ref.at[:, own], kb.at[mine_k], p["kp"] + j, partner)
    send(v_ref.at[:, own], vb.at[mine_k], p["vp"] + j, partner)
    gl_copy = local(g_ref, gl, p["gl"])

    w_copy.wait()
    for t in range(2):
        got(big.at[pl.ds(t * HD, HD)], p["big"] + t)
    feats = wb.shape[0]
    width = 2 * HD

    def project(f, carry):
        piece = at(f * width, width)
        xb[:, piece] = dot_nt(big[...], wb[piece, :])
        return carry

    cols_dev = big.shape[1]
    up_t = dot_nt(b_ref[:, at(c * cols_dev, cols_dev)], big[...])
    ls[0], ls[1] = up_t[:, :HD], up_t[:, HD:]
    send(ls.at[1 - c], lr, p["lora"], partner)
    lax.fori_loop(0, feats // width, project, 0)
    xs[...] = xb[at((1 - c) * HD, HD), :].astype(BF16)
    send(xs, xr, p["part"], partner)
    got(lr, p["lora"])
    up_mine = ls[c] + lr[...]
    lora = dot_nt((2.0 * up_mine).T.astype(BF16), a_ref[...])
    lub[half, :, at(j * HD, HD)] = up_mine.astype(BF16)
    for d in range(1, n):
        o, to = near(d)
        here = lub.at[half, :, at(j * HD, HD)]
        send(here, here, p["up"] + s, to)
    for d in range(n):
        o, to = far(d)
        here = lub.at[half, :, at(j * HD, HD)]
        send(here, here, p["up"] + s, to)
    got(xr, p["part"])
    dob[...] = (xb[rows, :] + xr[...].astype(F32) + lora).astype(BF16)
    for d in range(1, n):
        o, to = near(d)
        send(dob.at[:, at(o * 2 * HD, 2 * HD)], gb.at[mine_q], p["g"] + j, to)
    for d in range(n):
        o, to = far(d)
        send(dob.at[:, at(o * 2 * HD + HD, HD)], gr.at[mine_q], p["gx"] + j, to, when=late)
    gb[mine_q, :] = dob[:, own]

    for copy in own_copies:
        copy.wait()
    for d in range(1, n):
        o = lax.rem(j + d, n)
        block = at(o * 2 * HD + c * HD, HD)
        got(kb.at[block], p["k"] + o)
        send(kb.at[block], kb.at[block], p["kp"] + o, partner)
    for d in range(n):
        o = lax.rem(j + d, n)
        block = at(o * 2 * HD + c * HD, HD)

        @pl.when(late)
        def _():
            got(kr.at[block], p["kx"] + o)

        send(kr.at[block], kr.at[block], p["kxp"] + o, partner, when=late)
    for d in range(1, n):
        o = lax.rem(j + d, n)
        block = at(o * 2 * HD + c * HD, HD)
        got(vb.at[block], p["v"] + o)
        send(vb.at[block], vb.at[block], p["vp"] + o, partner)
    for d in range(n):
        o = lax.rem(j + d, n)
        block = at(o * 2 * HD + c * HD, HD)

        @pl.when(late)
        def _():
            got(vr.at[block], p["vx"] + o)

        send(vr.at[block], vr.at[block], p["vxp"] + o, partner, when=late)
    for d in range(1, n):
        o = lax.rem(j + d, n)
        got(qb.at[at(o * HD, HD)], p["q"] + o)
    for o in range(n):
        block = at(o * 2 * HD + (1 - c) * HD, HD)
        got(kb.at[block], p["kp"] + o)
        got(vb.at[block], p["vp"] + o)

    @pl.when(late)
    def _():
        for o in range(n):
            block = at(o * 2 * HD + (1 - c) * HD, HD)
            got(kr.at[block], p["kxp"] + o)
            got(vr.at[block], p["vxp"] + o)
        qr[...] = qb[:, :HD]

    @pl.when(early)
    def _():
        for o in range(n):
            got(qr.at[pl.ds(o * HD, HD)], p["qx"] + o)
        kr[...] = kb[:, HD:]
        vr[...] = vb[:, HD:]

    tile = 2 * HD
    total = kb.shape[0]
    lanes = (slice(0, HD), slice(HD, 2 * HD), slice(0, HD))
    keys, values = (kb, kb, kr), (vb, vb, vr)
    queries, douts = (qb, qb, qr), (gb, gb, gr)
    key_at = lax.broadcasted_iota(jnp.int32, (2 * tile, tile), 0)
    row = lax.broadcasted_iota(jnp.int32, (2 * tile, tile), 1)
    seen = key_at <= row + jnp.where(row >= HD, HD, 0) + c * HD

    def extent(part, u):
        return total if part == 2 else (u + 1) * 2 * tile

    tops, sums = [], []
    for part in range(3):
        kt[part] = keys[part][:, lanes[part]].T
        vt[part] = values[part][:, lanes[part]].T
        queries_t = queries[part][:, lanes[part]].T
        top_u, sum_u = [], []
        for u in range(2):
            ext = extent(part, u)
            q_t = queries_t[:, u * tile : (u + 1) * tile]
            scores = dot_nn(keys[part][:ext, lanes[part]], q_t)
            if part < 2:
                settled = ext - 2 * tile
                edge = jnp.where(seen, scores[settled:, :], NONE)
                scores = edge if settled == 0 else jnp.concatenate((scores[:settled, :], edge), axis=0)
            top = jnp.max(scores, axis=0, keepdims=True)
            powers = jnp.exp2((scores - top) * (SCALE * LOG2E))
            top_u.append(top)
            sum_u.append(jnp.sum(powers, axis=0, keepdims=True))
            low = powers.astype(BF16)
            probs[part, :ext, u * tile : (u + 1) * tile] = low
            ot[part, :, u * tile : (u + 1) * tile] = dot_nn(vt[part, :, :ext], low)
        tops.append(jnp.concatenate(top_u, axis=1))
        sums.append(jnp.concatenate(sum_u, axis=1))

    for d in range(1, n):
        o = lax.rem(j + d, n)
        got(gb.at[at(o * HD, HD)], p["g"] + o)

    @pl.when(late)
    def _():
        gr[...] = gb[:, :HD]

    @pl.when(early)
    def _():
        for o in range(n):
            got(gr.at[pl.ds(o * HD, HD)], p["gx"] + o)

    stats = []
    for part in range(3):
        g_t = douts[part][:, lanes[part]].astype(F32).T
        gt[part] = g_t
        stats.append((tops[part], sums[part], jnp.sum(ot[part] * g_t, axis=0, keepdims=True)))
    for r in range(3):
        stat_s[r : r + 1, :] = jnp.where(late, stats[1][r], stats[2][r])
    send(stat_s, stat_r, p["stat"], {"seq": (1 - half) * n + j})

    def choose(when_late, when_early):
        nothing = (NONE, 0.0, 0.0)
        one = when_late or nothing
        two = when_early or nothing
        return tuple(jnp.where(late, one[r], two[r]) for r in range(3))

    def backward(part, other):
        w, delta = combine(stats[part], other)
        delta = delta * w
        for u in reversed(range(2)):
            ext = extent(part, u)
            span = slice(u * tile, (u + 1) * tile)
            g_t = gt[part, :, span] * w[:, span]
            g = g_t.T.astype(BF16)
            low = probs[part, :ext, span]
            dprob = dot_nn(values[part][:ext, lanes[part]], g_t.astype(BF16))
            dscore = (dprob - delta[:, span]).astype(BF16) * low
            dq_t = dot_nn(kt[part, :, :ext], dscore)
            dq = (dq_t * SCALE).T
            dk = dot_nn(dscore, queries[part][span, lanes[part]])
            dv = dot_nn(low, g)
            at_k, at_v = 2 * part, 2 * part + 1
            if u == 1:
                acc[at_k], acc[at_v] = dk, dv
            else:
                acc[at_k, :ext, :] += dk
                acc[at_v, :ext, :] += dv
            dqs[part, span, :] = dq
        return w

    def to_partner(part, when=None):
        for t, scale in ((2 * part, SCALE), (2 * part + 1, 1.0)):
            for o in range(n):
                block = acc[t, at(o * 2 * HD + (1 - c) * HD, HD), :]
                ts[t, pl.ds(o * HD, HD), :] = (block * scale).astype(BF16)
            send(ts.at[t], tr.at[t], p["theirs"] + t, partner, when=when)

    outs = ((dk_out, "hk"), (dv_out, "hv"))

    def add_theirs(part):
        for t, scale in ((2 * part, SCALE), (2 * part + 1, 1.0)):
            got(tr.at[t], p["theirs"] + t)
            for o in range(n):
                span = pl.ds(o * HD, HD)
                block = acc[t, at(o * 2 * HD + c * HD, HD), :]
                hs[t, span, :] = (block * scale + tr[t, span, :].astype(F32)).astype(BF16)

    def go_home(part):
        add_theirs(part)
        cols = at(j * 2 * HD + part * HD, HD)
        for t, (out, name) in ((2 * part, outs[0]), (2 * part + 1, outs[1])):
            for d in range(1, n):
                o, to = near(d)
                send(hs.at[t, at(o * HD, HD)], out.at[:, cols], p[name] + part * n + j, to)
            out[:, cols] = hs[t, mine_q, :]

    dqh = {}

    def dq_home(part):
        cols = at(j * 2 * HD + part * HD, HD)
        for d in range(1, n):
            o, to = near(d)
            send(hs.at[6 + part, at(o * HD, HD)], dq_out.at[:, cols], p["hq"] + part * n + j, to)
        dq_out[:, cols] = hs[6 + part, mine_q, :]

    weights = [None] * 3
    weights[0] = backward(0, choose(stats[2], None))
    to_partner(0)
    got(stat_r, p["stat"])
    remote = tuple(stat_r[r : r + 1, :] for r in range(3))
    weights[2] = backward(2, choose(stats[0], remote))
    go_home(0)
    hs[6] = (dqs[0] + jnp.where(late, dqs[2], 0.0)).astype(BF16)
    dq_home(0)
    to_partner(2, when=late)

    @pl.when(early)
    def _():
        hs[8] = dqs[2].astype(BF16)

    for d in range(n):
        o, to = far(d)
        send(hs.at[8, at(o * HD, HD)], rq.at[j], p["rq"] + j, to, when=early)
    weights[1] = backward(1, choose(remote, None))
    for t in (0, 1):
        acc[2 + t] += jnp.where(early, acc[4 + t], 0.0)
    to_partner(1)
    hs[7] = dqs[1].astype(BF16)
    dq_home(1)

    @pl.when(late)
    def _():
        add_theirs(2)

    for t, name, to_ref in ((4, "rk", rk), (5, "rv", rv)):
        for d in range(n):
            o, to = far(d)
            send(hs.at[t, at(o * HD, HD)], to_ref.at[j], p[name] + j, to, when=late)

    attn = [(ot[part] * weights[part]).astype(BF16) for part in range(3)]
    for d in range(1, n):
        o = lax.rem(j + d, n)
        got(lub.at[half, :, at(o * HD, HD)], p["up"] + half * n + o)
    for d in range(n):
        o = lax.rem(j + d, n)
        got(lub.at[1 - half, :, at(o * HD, HD)], p["up"] + (1 - half) * n + o)
    down = [a_ref[at(j * 2 * HD + i * HD, HD), :].astype(F32).T.astype(BF16) for i in range(2)]
    here, there = lub[half], jnp.where(late, lub[half], lub[1 - half])
    mid_r = dot_nn(jnp.where(late, down[0], down[1]), attn[2])
    mid_here = dot_nn(down[0], attn[0]) + dot_nn(down[1], attn[1])
    ms[0] = mid_here + jnp.where(late, mid_r, 0.0)
    ms[1] = jnp.where(late, 0.0, mid_r)
    for d in range(1, n):
        o, to = near(d)
        send(ms.at[0, :, at(o * HD, HD)], mb.at[s], p["mid"] + s, to)
    for d in range(n):
        o, to = far(d)
        send(ms.at[1, :, at(o * HD, HD)], mb.at[s], p["mid"] + s, to)
    mb[s] = ms[0, :, at(j * HD, HD)]
    down_r = dot_nt(there, attn[2])
    dss[:, :HD] = dot_nt(here, attn[0]) + jnp.where(late, down_r, 0.0)
    dss[:, HD:] = dot_nt(here, attn[1]) + jnp.where(late, 0.0, down_r)
    send(dss, dsr, p["ds"], partner)
    go_home(1)
    for d in range(1, n):
        o = lax.rem(j + d, n)
        got(mb.at[half * n + o], p["mid"] + half * n + o)
    for d in range(n):
        o = lax.rem(j + d, n)
        got(mb.at[(1 - half) * n + o], p["mid"] + (1 - half) * n + o)
    mid = mb[0]
    for i in range(1, 2 * n):
        mid = mid + mb[i]
    mxs[...] = mid
    send(mxs, mxr, p["midx"], {"head": 1 - x})
    got(dsr, p["ds"])
    dnr[s] = 2.0 * (dss[...] + dsr[...])
    for d in range(1, 2 * n):
        other = lax.rem(s + d, 2 * n)
        send(dnr.at[s], dnr.at[s], p["dn"] + s, {"seq": other})
    gl_copy.wait()
    got(mxr, p["midx"])
    mid = (2.0 * (mid + mxr[...])).astype(BF16)
    up = dot_nn(mid, gl[...])
    side = us.shape[2]
    us[0], us[1] = up[:, :side], up[:, side:]
    send(us.at[1 - c], usr, p["us"], partner)
    got(usr, p["us"])
    us[c] += usr[...]
    for d in range(1, 2 * n):
        other = lax.rem(s + d, 2 * n)
        send(us.at[c, :, at(other * HD, HD)], urr.at[s], p["ur"] + s, {"seq": other})
    piece = us[c, :, at(s * HD, HD)]
    for d in range(1, 2 * n):
        other = lax.rem(s + d, 2 * n)
        got(urr.at[other], p["ur"] + other)
        piece = piece + urr[other]
    uf[c, :, at(s * HD, HD)] = piece
    for d in range(1, 2 * n):
        other = lax.rem(s + d, 2 * n)
        mine = uf.at[c, :, at(s * HD, HD)]
        send(mine, mine, p["ug"] + s, {"seq": other})
    for d in range(1, 2 * n):
        other = lax.rem(s + d, 2 * n)
        got(dnr.at[other], p["dn"] + other)
    for i in range(n):
        down_out[:, i * 2 * HD : (i + 1) * 2 * HD] = dnr[i] + dnr[i + n]
    for d in range(1, 2 * n):
        other = lax.rem(s + d, 2 * n)
        got(uf.at[c, :, at(other * HD, HD)], p["ug"] + other)
    send(uf.at[c], uf.at[c], p["uh"], partner)

    for part in range(2):
        for out, name in ((dq_out, "hq"), (dk_out, "hk"), (dv_out, "hv")):
            for d in range(1, n):
                o = lax.rem(j + d, n)
                got(out.at[:, at(o * 2 * HD + part * HD, HD)], p[name] + part * n + o)

    @pl.when(late)
    def _():
        for o in range(n):
            got(rq.at[o], p["rq"] + o)
            cols = slice(o * 2 * HD + HD, (o + 1) * 2 * HD)
            dq_out[:, cols] = (dq_out[:, cols].astype(F32) + rq[o].astype(F32)).astype(BF16)

    @pl.when(early)
    def _():
        for out, ref, name in ((dk_out, rk, "rk"), (dv_out, rv, "rv")):
            for o in range(n):
                got(ref.at[o], p[name] + o)
                cols = slice(o * 2 * HD, o * 2 * HD + HD)
                out[:, cols] = (out[:, cols].astype(F32) + ref[o].astype(F32)).astype(BF16)

    got(uf.at[1 - c], p["uh"])
    up_out[:, :side] = uf[0]
    up_out[:, side:] = uf[1]
    for copy, when in sends:
        if when is None:
            copy.wait_send()
        else:
            pl.when(when)(copy.wait_send)


def on_device_fused(q, k, v, g, w, a, b):
    rows, feats = q.shape
    cols = g.shape[1]
    rank = b.shape[0]
    tokens, window = BLOCKS * rows, 2 * BLOCKS * rows
    vmem, anywhere = pl.BlockSpec(memory_space=pltpu.VMEM), pl.BlockSpec(memory_space=pl.ANY)
    scratch = [
        ((tokens, 2 * HD), BF16), ((window, 2 * HD), BF16), ((window, 2 * HD), BF16), ((tokens, 2 * HD), BF16),
        ((tokens, HD), BF16), ((window, HD), BF16), ((window, HD), BF16), ((tokens, HD), BF16),
        ((2 * rows, cols), BF16), (w.shape, BF16), ((rows, cols), BF16), ((2 * rows, feats), F32),
        ((rows, feats), BF16), ((rows, feats), BF16), ((2, rank, rows), F32), ((rank, rows), F32),
        ((2, rank, tokens), BF16), ((rows, feats), BF16),
        ((3, HD, window), BF16), ((3, HD, window), BF16), ((3, window, tokens), BF16), ((3, HD, tokens), F32),
        ((3, HD, tokens), F32), ((6, window, HD), F32), ((8, tokens), F32), ((8, tokens), F32),
        ((6, tokens, HD), BF16), ((6, tokens, HD), BF16), ((9, tokens, HD), BF16), ((3, tokens, HD), F32),
        ((BLOCKS, rows, HD), BF16), ((BLOCKS, rows, HD), BF16), ((BLOCKS, rows, HD), BF16),
        ((2, rank, tokens), F32), ((2 * BLOCKS, rank, rows), F32), ((rank, rows), F32), ((rank, rows), F32),
        ((2, rank, cols // 2), F32), ((rank, cols // 2), F32), ((2 * BLOCKS, rank, HD), F32),
        ((2, rank, cols // 2), F32), ((rank, 2 * HD), F32), ((rank, 2 * HD), F32), ((2 * BLOCKS, rank, 2 * HD), F32),
    ]
    dq, dk, dv, down, up = pl.pallas_call(
        fused_kernel,
        out_shape=(
            jax.ShapeDtypeStruct((rows, feats), BF16),
            jax.ShapeDtypeStruct((rows, feats), BF16),
            jax.ShapeDtypeStruct((rows, feats), BF16),
            jax.ShapeDtypeStruct((rank, feats), F32),
            jax.ShapeDtypeStruct((rank, cols), F32),
        ),
        in_specs=[anywhere] * 5 + [vmem] * 2,
        out_specs=[vmem] * 5,
        scratch_shapes=[pltpu.VMEM(shape, kind) for shape, kind in scratch]
        + [pltpu.SemaphoreType.DMA((SENDS,)), pltpu.SemaphoreType.DMA((RECEIVES,))],
        compiler_params=pltpu.CompilerParams(
            collective_id=0, has_side_effects=True, vmem_limit_bytes=48 * 1024 * 1024
        ),
    )(q, k, v, g, w, a, b)
    return dq, dk, dv, down.T, up


def one_group(mesh, rows, feats, width):
    seq, head, sub = mesh.shape["seq"], mesh.shape["head"], mesh.shape["sub"]
    return (
        sub == 2
        and head == 2
        and rows == HD
        and seq == 2 * BLOCKS
        and seq * sub * rows == GROUP
        and feats == seq * HD
        and width == 2 * seq * HD
    )


def solution(mesh):
    in_specs = (
        P(("rep", "seq", "sub"), "head"),
        P(("rep", "seq", "sub"), "head"),
        P(("rep", "seq", "sub"), "head"),
        P(("rep", "seq", "sub"), "head"),
        P("head", "sub"),
        P("head", None),
        P(),
    )
    out_specs = (
        P(("rep", "seq", "sub"), "head"),
        P(("rep", "seq", "sub"), "head"),
        P(("rep", "seq", "sub"), "head"),
        P(("rep", "head"), None),
        P("rep", "head"),
    )

    def on_device(*local):
        if one_group(mesh, *local[0].shape, local[3].shape[1]):
            return on_device_fused(*local)
        return on_device_windows(*local)

    return jax.shard_map(
        on_device, mesh=mesh, in_specs=in_specs, out_specs=out_specs, check_vma=False
    )
```

```python
import jax
import jax.numpy as jnp
from jax import lax
from jax.experimental import pallas as pl
from jax.experimental.pallas import tpu as pltpu
from jax.sharding import PartitionSpec as P

HD = 128
GROUP = 2048


def passed_along(value, axis, by):
    peers = lax.axis_size(axis)
    return lax.ppermute(value, axis, [(i, (i + by) % peers) for i in range(peers)])


def placed_visible(row_count, window_rows, seq_total, first_row, back_rows, roll_by):
    query_pos = first_row + lax.broadcasted_iota(jnp.int32, (row_count, window_rows), 0)
    key_pos = (
        first_row
        - back_rows
        + seq_total
        + lax.broadcasted_iota(jnp.int32, (row_count, window_rows), 1)
    ) % seq_total
    query_order = (query_pos - roll_by + seq_total) % seq_total
    key_order = (key_pos - roll_by + seq_total) % seq_total
    return (query_order // GROUP == key_order // GROUP) & (key_order <= query_order)


def softmax_rows(query_head, keys_head, visible):
    scores = lax.dot_general(
        query_head, keys_head, (((1,), (1,)), ((), ())), preferred_element_type=jnp.float32
    )
    scores = jnp.where(visible, scores * HD ** (-0.5), -jnp.inf)
    highest = jnp.max(scores, axis=1, keepdims=True)
    powers = jnp.exp(scores - highest)
    return powers / jnp.sum(powers, axis=1, keepdims=True)


def head_forward(query_head, window_head, visible):
    prob = softmax_rows(query_head, window_head[0], visible)
    return jnp.dot(
        prob.astype(jnp.bfloat16), window_head[1], preferred_element_type=jnp.float32
    ).astype(jnp.bfloat16)


def head_backward(query_head, window_head, dout_head, visible):
    prob = softmax_rows(query_head, window_head[0], visible)
    prob_lo = prob.astype(jnp.bfloat16)
    dprob = lax.dot_general(
        dout_head, window_head[1], (((1,), (1,)), ((), ())), preferred_element_type=jnp.float32
    )
    delta = jnp.sum(prob * dprob, axis=1, keepdims=True)
    dscore = (prob * (dprob - delta) * HD ** (-0.5)).astype(jnp.bfloat16)
    grad_q = jnp.dot(dscore, window_head[0], preferred_element_type=jnp.float32).astype(
        jnp.bfloat16
    )
    grad_k = lax.dot_general(
        dscore, query_head, (((0,), (0,)), ((), ())), preferred_element_type=jnp.float32
    )
    grad_v = lax.dot_general(
        prob_lo, dout_head, (((0,), (0,)), ((), ())), preferred_element_type=jnp.float32
    )
    return (grad_q, jnp.stack((grad_k.astype(jnp.bfloat16), grad_v.astype(jnp.bfloat16))))


def attend_window(query_rows, window, dout_rows, visible):
    row_count, feat_count = query_rows.shape
    heads_here = feat_count // HD
    window_rows = window.shape[1]
    window_heads = window.reshape(2, window_rows, heads_here, HD).transpose(2, 0, 1, 3)
    query_heads = query_rows.reshape(row_count, heads_here, HD).transpose(1, 0, 2)
    dout_heads = dout_rows.reshape(row_count, heads_here, HD).transpose(1, 0, 2)
    attn_heads = lax.map(
        lambda pieces: head_forward(pieces[0], pieces[1], visible), (query_heads, window_heads)
    )
    grad_q_heads, pair_heads = lax.map(
        lambda pieces: head_backward(pieces[0], pieces[1], pieces[2], visible),
        (query_heads, window_heads, dout_heads),
    )
    attention_output = attn_heads.transpose(1, 0, 2).reshape(row_count, feat_count)
    query_gradient = grad_q_heads.transpose(1, 0, 2).reshape(row_count, feat_count)
    pair_grads = pair_heads.transpose(1, 2, 0, 3).reshape(2, window_rows, feat_count)
    return (attention_output, query_gradient, pair_grads)


def on_device_windows(
    head_query_rows,
    head_key_rows,
    head_value_rows,
    output_gradient,
    output_matrix,
    adapter_down_weight,
    adapter_up_weight,
):
    tokens_dev, feat_dev = head_query_rows.shape
    head_index = lax.axis_index("head")
    shifted = head_index >= lax.axis_size("head") // 2
    total_gradient = lax.all_gather(output_gradient, "head", axis=1, tiled=True)
    projected_output = lax.dot_general(
        total_gradient,
        lax.all_gather(output_matrix, "sub", axis=1, tiled=True),
        (((1,), (1,)), ((), ())),
        preferred_element_type=jnp.float32,
    )
    adapter_upward = lax.dot_general(
        total_gradient,
        adapter_up_weight,
        (((1,), (1,)), ((), ())),
        preferred_element_type=jnp.float32,
    )
    adapter_backward = jnp.dot(
        adapter_upward, adapter_down_weight.astype(jnp.float32).T, precision=lax.Precision.HIGHEST
    )
    attention_gradient = (projected_output + 2.0 * adapter_backward).astype(jnp.bfloat16)
    sub_count = lax.axis_size("sub")
    block_rows = tokens_dev * sub_count
    seq_total = block_rows * lax.axis_size("seq")
    reach = max(GROUP // block_rows - 1, 1)
    roll_by = jnp.where(shifted, GROUP // 2, 0)
    stacked = jnp.stack((head_query_rows, head_key_rows, head_value_rows, attention_gradient))
    moved = lax.all_to_all(stacked, "sub", split_axis=2, concat_axis=1, tiled=True)
    own_pair = moved[1:3]
    received = [passed_along(own_pair, "seq", distance) for distance in range(reach, 0, -1)]
    window = jnp.concatenate(received + [own_pair], axis=1)
    first_row = lax.axis_index("seq") * block_rows
    visible = placed_visible(
        block_rows, window.shape[1], seq_total, first_row, reach * block_rows, roll_by
    )
    attn_local, grad_q_local, pair_grads = attend_window(moved[0], window, moved[3], visible)
    running = pair_grads[:, reach * block_rows :].astype(jnp.float32)
    for distance in range(1, reach + 1):
        begin_row = (reach - distance) * block_rows
        block_terms = pair_grads[:, begin_row : begin_row + block_rows]
        returned = passed_along(block_terms, "seq", -distance)
        running = running + returned.astype(jnp.float32)
    pair_local = running.astype(jnp.bfloat16)
    back = jnp.stack((attn_local, grad_q_local, pair_local[0], pair_local[1]))
    restored = lax.all_to_all(back, "sub", split_axis=1, concat_axis=2, tiled=True)
    attention_output = restored[0]
    query_gradient = restored[1]
    key_gradient = restored[2]
    value_gradient = restored[3]
    middle_piece = jnp.dot(
        attention_output, adapter_down_weight, preferred_element_type=jnp.float32
    )
    down_gradient_part = 2.0 * jnp.dot(
        attention_output.astype(jnp.float32).T, adapter_upward, precision=lax.Precision.HIGHEST
    )
    adapter_middle = lax.psum(middle_piece, "head")
    up_gradient_part = 2.0 * jnp.dot(
        adapter_middle.T, output_gradient.astype(jnp.float32), precision=lax.Precision.HIGHEST
    )
    adapter_down_gradient, adapter_up_gradient = lax.psum(
        (down_gradient_part, up_gradient_part), ("seq", "sub")
    )
    return (
        query_gradient,
        key_gradient,
        value_gradient,
        adapter_down_gradient,
        adapter_up_gradient,
    )


SCALE = HD ** (-0.5)
F32, BF16 = jnp.float32, jnp.bfloat16


def dot_nn(left, right):
    return lax.dot_general(left, right, (((1,), (0,)), ((), ())), preferred_element_type=F32)


def dot_nt(left, right):
    return lax.dot_general(left, right, (((1,), (1,)), ((), ())), preferred_element_type=F32)


MESH = pl.DeviceIdType.MESH
BLOCKS = 4
CUTS = 2
PIECES = 1
LOG2E = 1.4426950408889634
NONE = -1e30


class Slots:
    def __init__(self):
        self.count = 0

    def take(self, many=1):
        first = self.count
        self.count += many
        return first


def make_slots():
    names = dict(
        k=4, q=4, v=4, g=4 * CUTS, kx=4, vx=4, qx=4, gx=4 * CUTS, kp=4, vp=4, kxp=4, vxp=4, big=2 * CUTS, w=1, gl=1, a=1, b=1,
        part=CUTS, lora=CUTS, up=8, stat=1, share=1, theirs=6, hq=8, hk=8, hv=8, rq=4, rk=4, rv=4,
        mid=8, midx=1, us=1, ur=8, ug=8, uh=1, ds=1, dn=8,
    )
    slots, places = Slots(), {}
    for name, many in names.items():
        places[name] = slots.take(many)
    return places, slots.count


PLACES, RECEIVES = make_slots()
SENDS = 192


def combine(mine, other):
    top = jnp.maximum(mine[0], other[0])
    c = SCALE * LOG2E
    e1, e2 = jnp.exp2((mine[0] - top) * c), jnp.exp2((other[0] - top) * c)
    w = 1.0 / (mine[1] * e1 + other[1] * e2)
    return e1 * w, e2 * w


def fused_kernel(
    q_ref, k_ref, v_ref, g_ref, w_ref, a_hbm, b_hbm,
    dq_out, dk_out, dv_out, down_out, up_out,
    qb, kb, vb, gb, qr, kr, vr, gr,
    a_ref, b_ref, big, wb, gl, xb, xs, xr, ls, lr, lt, lub, dob,
    kt, vt, probs, ot, gt, acc, stat_s, stat_r, share_s, share_r, ts, tr, hs, dqs,
    rk, rv, rq, ms, mb, mf, mxs, mxr, us, usr, urr, uf, dss, dsr, dnr,
    ssem, rsem,
):
    s, x, c = lax.axis_index("seq"), lax.axis_index("head"), lax.axis_index("sub")
    n = BLOCKS
    half, j = s // n, lax.rem(s, n)
    late = lax.rem(half + x, 2) == 1
    early = lax.rem(half + x, 2) == 0
    partner = {"sub": 1 - c}
    sends = []
    counter = Slots()

    def at(base, many):
        return pl.ds(pl.multiple_of(base, many), many)

    def send(src, dst, place, to, when=None):
        copy = pltpu.make_async_remote_copy(
            src_ref=src, dst_ref=dst, send_sem=ssem.at[counter.take()], recv_sem=rsem.at[place],
            device_id=to, device_id_type=MESH,
        )
        if when is None:
            copy.start()
        else:
            pl.when(when)(copy.start)
        sends.append((copy, when))

    def got(dst, place):
        pltpu.make_async_remote_copy(
            src_ref=dst, dst_ref=dst, send_sem=ssem.at[0], recv_sem=rsem.at[place],
            device_id=partner, device_id_type=MESH,
        ).wait_recv()

    def local(src, dst, place):
        copy = pltpu.make_async_copy(src, dst, rsem.at[place])
        copy.start()
        return copy

    def near(d):
        o = lax.rem(j + d, n)
        return o, {"seq": half * n + o}

    def far(d):
        o = lax.rem(j + d, n)
        return o, {"seq": (1 - half) * n + o}

    p = PLACES
    barrier = pltpu.get_barrier_semaphore()
    greeted = [near(d)[1] for d in range(1, n)] + [far(d)[1] for d in range(n)]
    greeted += [partner, {"head": 1 - x}, {"head": 1 - x, "sub": 1 - c}]
    for device in greeted:
        pl.semaphore_signal(barrier, inc=1, device_id=device, device_id_type=MESH)
    pl.semaphore_wait(barrier, len(greeted))

    part_rows = HD // CUTS
    for r in range(CUTS):
        mine_g = at(r * 2 * part_rows + c * part_rows, part_rows)
        from_g = g_ref.at[pl.ds(r * part_rows, part_rows)]
        place = p["big"] + r * 2 + c
        send(from_g, big.at[mine_g], place, {"head": 1 - x, "sub": x})
        send(from_g, big.at[mine_g], place, partner, when=c != x)

        @pl.when(c == x)
        def _():
            local(from_g, big.at[mine_g], place)

    w_copy = local(w_ref, wb, p["w"])
    low_rank_copies = [local(a_hbm, a_ref, p["a"]), local(b_hbm, b_ref, p["b"])]
    mine_k, mine_q = at(j * 2 * HD + c * HD, HD), at(j * HD, HD)
    for d in range(1, n):
        o, to = near(d)
        cols = at(o * 2 * HD, 2 * HD)
        send(k_ref.at[:, cols], kb.at[mine_k], p["k"] + j, to)
        send(q_ref.at[:, cols], qb.at[mine_q], p["q"] + j, to)
    for d in range(n):
        o, to = far(d)
        first, second = at(o * 2 * HD, HD), at(o * 2 * HD + HD, HD)
        send(k_ref.at[:, first], kr.at[mine_k], p["kx"] + j, to, when=early)
        send(q_ref.at[:, second], qr.at[mine_q], p["qx"] + j, to, when=late)
    for d in range(1, n):
        o, to = near(d)
        send(v_ref.at[:, at(o * 2 * HD, 2 * HD)], vb.at[mine_k], p["v"] + j, to)
    for d in range(n):
        o, to = far(d)
        send(v_ref.at[:, at(o * 2 * HD, HD)], vr.at[mine_k], p["vx"] + j, to, when=early)
    own = at(j * 2 * HD, 2 * HD)
    own_copies = [
        local(k_ref.at[:, own], kb.at[mine_k], p["k"] + j),
        local(v_ref.at[:, own], vb.at[mine_k], p["v"] + j),
        local(q_ref.at[:, own], qb.at[mine_q], p["q"] + j),
    ]
    send(k_ref.at[:, own], kb.at[mine_k], p["kp"] + j, partner)
    send(v_ref.at[:, own], vb.at[mine_k], p["vp"] + j, partner)
    gl_copy = local(g_ref, gl, p["gl"])

    w_copy.wait()
    for copy in low_rank_copies:
        copy.wait()
    feats, cols_dev, width = wb.shape[0], big.shape[1], 2 * HD
    ups = []
    for r in range(CUTS):
        for t in range(2):
            got(big.at[pl.ds((2 * r + t) * part_rows, part_rows)], p["big"] + r * 2 + t)
        both = pl.ds(r * 2 * part_rows, 2 * part_rows)

        def project(f, carry):
            piece = at(f * width, width)
            xb[both, piece] = dot_nt(big[both, :], wb[piece, :])
            return carry

        ls[r] = dot_nt(b_ref[:, at(c * cols_dev, cols_dev)], big[both, :])
        send(ls.at[r], lr.at[r], p["lora"] + r, partner)
        lax.fori_loop(0, feats // width, project, 0)
        span = pl.ds(r * part_rows, part_rows)
        xs[span, :] = xb[at((2 * r + 1 - c) * part_rows, part_rows), :].astype(BF16)
        send(xs.at[span], xr.at[span], p["part"] + r, partner)
        got(lr.at[r], p["lora"] + r)
        up_r = ls[r] + lr[r]
        lt[...] = (2.0 * up_r).T
        ups.append(up_r)
        lora = dot_nn(lt[at(c * part_rows, part_rows), :].astype(BF16), a_ref[...])
        got(xr.at[span], p["part"] + r)
        own_x = xb[at((2 * r + c) * part_rows, part_rows), :]
        dob[span, :] = (own_x + xr[span, :].astype(F32) + lora).astype(BF16)
        mine_d = at(j * HD + r * part_rows, part_rows)
        for d in range(1, n):
            o, to = near(d)
            send(dob.at[span, at(o * 2 * HD, 2 * HD)], gb.at[mine_d], p["g"] + r * n + j, to)
        for d in range(n):
            o, to = far(d)
            send(dob.at[span, at(o * 2 * HD + HD, HD)], gr.at[mine_d], p["gx"] + r * n + j, to, when=late)
    gb[mine_q, :] = dob[:, own]
    up_mine = jnp.where(
        c == 0,
        jnp.concatenate([u[:, :part_rows] for u in ups], axis=1),
        jnp.concatenate([u[:, part_rows:] for u in ups], axis=1),
    )
    here = lub.at[half, :, at(j * HD, HD)]
    lub[half, :, at(j * HD, HD)] = up_mine.astype(BF16)
    for d in range(1, n):
        o, to = near(d)
        send(here, here, p["up"] + s, to)
    for d in range(n):
        o, to = far(d)
        send(here, here, p["up"] + s, to)

    for copy in own_copies:
        copy.wait()
    for d in range(1, n):
        o = lax.rem(j + d, n)
        block = at(o * 2 * HD + c * HD, HD)
        got(kb.at[block], p["k"] + o)
        send(kb.at[block], kb.at[block], p["kp"] + o, partner)
    for d in range(n):
        o = lax.rem(j + d, n)
        block = at(o * 2 * HD + c * HD, HD)

        @pl.when(late)
        def _():
            got(kr.at[block], p["kx"] + o)

        send(kr.at[block], kr.at[block], p["kxp"] + o, partner, when=late)
    for d in range(1, n):
        o = lax.rem(j + d, n)
        block = at(o * 2 * HD + c * HD, HD)
        got(vb.at[block], p["v"] + o)
        send(vb.at[block], vb.at[block], p["vp"] + o, partner)
    for d in range(n):
        o = lax.rem(j + d, n)
        block = at(o * 2 * HD + c * HD, HD)

        @pl.when(late)
        def _():
            got(vr.at[block], p["vx"] + o)

        send(vr.at[block], vr.at[block], p["vxp"] + o, partner, when=late)
    for d in range(1, n):
        o = lax.rem(j + d, n)
        got(qb.at[at(o * HD, HD)], p["q"] + o)
    for o in range(n):
        block = at(o * 2 * HD + (1 - c) * HD, HD)
        got(kb.at[block], p["kp"] + o)
        got(vb.at[block], p["vp"] + o)

    @pl.when(late)
    def _():
        for o in range(n):
            block = at(o * 2 * HD + (1 - c) * HD, HD)
            got(kr.at[block], p["kxp"] + o)
            got(vr.at[block], p["vxp"] + o)
        qr[...] = qb[:, :HD]

    @pl.when(early)
    def _():
        for o in range(n):
            got(qr.at[pl.ds(o * HD, HD)], p["qx"] + o)
        kr[...] = kb[:, HD:]
        vr[...] = vb[:, HD:]

    tile = 2 * HD
    total = kb.shape[0]
    lanes = (slice(0, HD), slice(HD, 2 * HD), slice(0, HD))
    keys, values = (kb, kb, kr), (vb, vb, vr)
    queries, douts = (qb, qb, qr), (gb, gb, gr)
    key_at = lax.broadcasted_iota(jnp.int32, (2 * tile, tile), 0)
    row = lax.broadcasted_iota(jnp.int32, (2 * tile, tile), 1)
    seen = key_at <= row + jnp.where(row >= HD, HD, 0) + c * HD

    def extent(part, u):
        return total if part == 2 else (u + 1) * 2 * tile

    tops, sums = [], []
    for part in range(3):
        kt[part] = keys[part][:, lanes[part]].T
        vt[part] = values[part][:, lanes[part]].T
        queries_t = queries[part][:, lanes[part]].T
        top_u, sum_u = [], []
        for u in range(2):
            ext = extent(part, u)
            q_t = queries_t[:, u * tile : (u + 1) * tile]
            scores = dot_nn(keys[part][:ext, lanes[part]], q_t)
            if part < 2:
                settled = ext - 2 * tile
                edge = jnp.where(seen, scores[settled:, :], NONE)
                scores = edge if settled == 0 else jnp.concatenate((scores[:settled, :], edge), axis=0)
            top = jnp.max(scores, axis=0, keepdims=True)
            powers = jnp.exp2((scores - top) * (SCALE * LOG2E))
            top_u.append(top)
            sum_u.append(jnp.sum(powers, axis=0, keepdims=True))
            low = powers.astype(BF16)
            probs[part, :ext, u * tile : (u + 1) * tile] = low
            ot[part, :, u * tile : (u + 1) * tile] = dot_nn(vt[part, :, :ext], low)
        tops.append(jnp.concatenate(top_u, axis=1))
        sums.append(jnp.concatenate(sum_u, axis=1))

    local_stats = [(tops[part], sums[part]) for part in range(3)]
    for r in range(2):
        stat_s[r : r + 1, :] = jnp.where(late, local_stats[1][r], local_stats[2][r])
    nothing = (NONE, 0.0)
    other_0 = tuple(jnp.where(late, local_stats[2][r], nothing[r]) for r in range(2))
    first, second = combine(local_stats[0], other_0)
    attn_0 = (ot[0] * first + jnp.where(late, ot[2] * second, 0.0)).astype(BF16)
    down = [a_ref[:, at(j * 2 * HD + i * HD, HD)] for i in range(2)]
    alone = ot[1] * jnp.where(late, 1.0, 1.0 / sums[1])
    mid_0, mid_1 = dot_nn(down[0], attn_0), dot_nn(down[1], alone.astype(BF16))
    rank = mid_0.shape[0]
    ms[:rank, :] = mid_0 + jnp.where(late, 0.0, mid_1)
    ms[rank : 2 * rank, :] = jnp.where(late, mid_1, dot_nn(down[1], ot[2].astype(BF16)))
    ms[2 * rank :, :] = stat_s[...]
    for d in range(1, n):
        o, to = near(d)
        send(ms.at[:, at(o * HD, HD)], mb.at[j], p["mid"] + j, to)
    for d in range(n):
        o, to = far(d)
        send(ms.at[pl.ds(rank, rank + 8), at(o * HD, HD)], mf.at[j], p["mid"] + n + j, to, when=early)
    mb[j] = ms[:, at(j * HD, HD)]
    send(stat_s, stat_r, p["stat"], {"seq": (1 - half) * n + j})
    for d in range(1, n):
        o = lax.rem(j + d, n)
        for r in range(CUTS):
            got(gb.at[at(o * HD + r * part_rows, part_rows)], p["g"] + r * n + o)

    @pl.when(late)
    def _():
        gr[...] = gb[:, :HD]

    @pl.when(early)
    def _():
        for o in range(n):
            for r in range(CUTS):
                got(gr.at[pl.ds(o * HD + r * part_rows, part_rows)], p["gx"] + r * n + o)

    shares = []
    for part in range(3):
        g_t = douts[part][:, lanes[part]].astype(F32).T
        gt[part] = g_t
        shares.append(jnp.sum(ot[part] * g_t, axis=0, keepdims=True))
    share_s[...] = jnp.broadcast_to(jnp.where(late, shares[1], shares[2]), share_s.shape)
    send(share_s, share_r, p["share"], {"seq": (1 - half) * n + j})
    for d in range(1, n):
        o = lax.rem(j + d, n)
        got(mb.at[o], p["mid"] + o)
    mid = mb[0, :rank, :]
    for o in range(1, n):
        mid = mid + mb[o, :rank, :]
    mxs[...] = mid

    @pl.when(late)
    def _():
        whole = mxs[...]
        for o in range(n):
            got(mf.at[o], p["mid"] + n + o)
            near_stat = (mb[o, 2 * rank : 2 * rank + 1, :], mb[o, 2 * rank + 1 : 2 * rank + 2, :])
            far_stat = (mf[o, rank : rank + 1, :], mf[o, rank + 1 : rank + 2, :])
            w_near, w_far = combine(near_stat, far_stat)
            whole = whole + mb[o, rank : 2 * rank, :] * w_near + mf[o, :rank, :] * w_far
        mxs[...] = whole

    send(mxs, mxr, p["midx"], {"head": 1 - x})
    got(stat_r, p["stat"])
    remote = (stat_r[0:1, :], stat_r[1:2, :])
    other_1 = tuple(jnp.where(late, remote[r], nothing[r]) for r in range(2))
    other_2 = tuple(jnp.where(late, local_stats[0][r], remote[r]) for r in range(2))
    weights = [(first, second), combine(local_stats[1], other_1), combine(local_stats[2], other_2)]
    attn_1 = (ot[1] * weights[1][0]).astype(BF16)
    attn_2 = (ot[2] * weights[2][0]).astype(BF16)
    for d in range(1, n):
        o = lax.rem(j + d, n)
        got(lub.at[half, :, at(o * HD, HD)], p["up"] + half * n + o)
    for d in range(n):
        o = lax.rem(j + d, n)
        got(lub.at[1 - half, :, at(o * HD, HD)], p["up"] + (1 - half) * n + o)
    near_up = lub[half]
    dss[:, :HD] = dot_nt(near_up, attn_0)
    dss[:, HD:] = dot_nt(near_up, attn_1) + jnp.where(late, 0.0, dot_nt(lub[1 - half], attn_2))
    send(dss, dsr, p["ds"], partner)

    def backward(part, other):
        w, w_other = weights[part]
        delta = (w * shares[part] + w_other * other) * w
        for u in reversed(range(2)):
            ext = extent(part, u)
            span = slice(u * tile, (u + 1) * tile)
            g_t = gt[part, :, span] * w[:, span]
            g = g_t.T.astype(BF16)
            low = probs[part, :ext, span]
            dprob = dot_nn(values[part][:ext, lanes[part]], g_t.astype(BF16))
            dscore = (dprob - delta[:, span]).astype(BF16) * low
            dq_t = dot_nn(kt[part, :, :ext], dscore)
            dq = (dq_t * SCALE).T
            dk = dot_nn(dscore, queries[part][span, lanes[part]])
            dv = dot_nn(low, g)
            at_k, at_v = 2 * part, 2 * part + 1
            if u == 1:
                acc[at_k], acc[at_v] = dk, dv
            else:
                acc[at_k, :ext, :] += dk
                acc[at_v, :ext, :] += dv
            dqs[part, span, :] = dq

    def to_partner(part, when=None):
        for t, scale in ((2 * part, SCALE), (2 * part + 1, 1.0)):
            for o in range(n):
                block = acc[t, at(o * 2 * HD + (1 - c) * HD, HD), :]
                ts[t, pl.ds(o * HD, HD), :] = (block * scale).astype(BF16)
            send(ts.at[t], tr.at[t], p["theirs"] + t, partner, when=when)

    outs = ((dk_out, "hk"), (dv_out, "hv"))

    def add_theirs(part):
        for t, scale in ((2 * part, SCALE), (2 * part + 1, 1.0)):
            got(tr.at[t], p["theirs"] + t)
            for o in range(n):
                span = pl.ds(o * HD, HD)
                block = acc[t, at(o * 2 * HD + c * HD, HD), :]
                hs[t, span, :] = (block * scale + tr[t, span, :].astype(F32)).astype(BF16)

    def home_sends(part, t):
        cols = at(j * 2 * HD + part * HD, HD)
        out, name = outs[t % 2]
        for d in range(1, n):
            o, to = near(d)
            send(hs.at[t, at(o * HD, HD)], out.at[:, cols], p[name] + part * n + j, to)
        out[:, cols] = hs[t, mine_q, :]

    def dq_home(part):
        cols = at(j * 2 * HD + part * HD, HD)
        for d in range(1, n):
            o, to = near(d)
            send(hs.at[6 + part, at(o * HD, HD)], dq_out.at[:, cols], p["hq"] + part * n + j, to)
        dq_out[:, cols] = hs[6 + part, mine_q, :]

    backward(0, jnp.where(late, shares[2], 0.0))
    to_partner(0)
    got(dsr, p["ds"])
    dnr[s] = 2.0 * (dss[...] + dsr[...])
    for d in range(1, 2 * n):
        other = lax.rem(s + d, 2 * n)
        send(dnr.at[s], dnr.at[s], p["dn"] + s, {"seq": other})
    gl_copy.wait()
    got(mxr, p["midx"])
    mid = (2.0 * (mxs[...] + mxr[...])).astype(BF16)
    up = dot_nn(mid, gl[...])
    side = us.shape[2]
    us[0], us[1] = up[:, :side], up[:, side:]
    send(us.at[1 - c], usr, p["us"], partner)
    got(share_r, p["share"])
    far_share = share_r[0:1, :]
    backward(2, jnp.where(late, shares[0], far_share))
    add_theirs(0)
    home_sends(0, 0)
    home_sends(0, 1)
    hs[6] = (dqs[0] + jnp.where(late, dqs[2], 0.0)).astype(BF16)
    dq_home(0)
    to_partner(2, when=late)

    @pl.when(early)
    def _():
        hs[8] = dqs[2].astype(BF16)

    for d in range(n):
        o, to = far(d)
        send(hs.at[8, at(o * HD, HD)], rq.at[j], p["rq"] + j, to, when=early)
    got(usr, p["us"])
    us[c] += usr[...]
    for d in range(1, 2 * n):
        other = lax.rem(s + d, 2 * n)
        send(us.at[c, :, at(other * HD, HD)], urr.at[s], p["ur"] + s, {"seq": other})
    backward(1, jnp.where(late, far_share, 0.0))
    for t in (0, 1):
        acc[2 + t] += jnp.where(early, acc[4 + t], 0.0)
    to_partner(1)
    hs[7] = dqs[1].astype(BF16)
    dq_home(1)

    @pl.when(late)
    def _():
        add_theirs(2)

    for t, name, to_ref in ((4, "rk", rk), (5, "rv", rv)):
        for d in range(n):
            o, to = far(d)
            send(hs.at[t, at(o * HD, HD)], to_ref.at[j], p[name] + j, to, when=late)

    add_theirs(1)
    home_sends(1, 2)
    piece = us[c, :, at(s * HD, HD)]
    for d in range(1, 2 * n):
        other = lax.rem(s + d, 2 * n)
        got(urr.at[other], p["ur"] + other)
        piece = piece + urr[other]
    uf[c, :, at(s * HD, HD)] = piece
    for d in range(1, 2 * n):
        other = lax.rem(s + d, 2 * n)
        mine = uf.at[c, :, at(s * HD, HD)]
        send(mine, mine, p["ug"] + s, {"seq": other})
    home_sends(1, 3)
    for d in range(1, 2 * n):
        other = lax.rem(s + d, 2 * n)
        got(dnr.at[other], p["dn"] + other)
    for i in range(n):
        down_out[:, i * 2 * HD : (i + 1) * 2 * HD] = dnr[i] + dnr[i + n]
    for d in range(1, 2 * n):
        other = lax.rem(s + d, 2 * n)
        got(uf.at[c, :, at(other * HD, HD)], p["ug"] + other)
    send(uf.at[c], uf.at[c], p["uh"], partner)

    for part in range(2):
        for out, name in ((dq_out, "hq"), (dk_out, "hk"), (dv_out, "hv")):
            for d in range(1, n):
                o = lax.rem(j + d, n)
                got(out.at[:, at(o * 2 * HD + part * HD, HD)], p[name] + part * n + o)

    @pl.when(late)
    def _():
        for o in range(n):
            got(rq.at[o], p["rq"] + o)
            cols = slice(o * 2 * HD + HD, (o + 1) * 2 * HD)
            dq_out[:, cols] = (dq_out[:, cols].astype(F32) + rq[o].astype(F32)).astype(BF16)

    @pl.when(early)
    def _():
        for out, ref, name in ((dk_out, rk, "rk"), (dv_out, rv, "rv")):
            for o in range(n):
                got(ref.at[o], p[name] + o)
                cols = slice(o * 2 * HD, o * 2 * HD + HD)
                out[:, cols] = (out[:, cols].astype(F32) + ref[o].astype(F32)).astype(BF16)

    got(uf.at[1 - c], p["uh"])
    up_out[:, :side] = uf[0]
    up_out[:, side:] = uf[1]
    for copy, when in sends:
        if when is None:
            copy.wait_send()
        else:
            pl.when(when)(copy.wait_send)


def written(*arrays):
    def kernel(*refs):
        copies = []
        for i, array in enumerate(arrays):
            rows = array.shape[0] // PIECES
            for k in range(PIECES):
                piece = pl.ds(k * rows, rows)
                copies.append(
                    pltpu.make_async_copy(
                        refs[i].at[piece], refs[len(arrays) + i].at[piece], refs[-1].at[i, k]
                    )
                )
        for copy in copies:
            copy.start()
        for copy in copies:
            copy.wait()

    return pl.pallas_call(
        kernel,
        out_shape=tuple(jax.ShapeDtypeStruct(array.shape, array.dtype) for array in arrays),
        in_specs=[pl.BlockSpec(memory_space=pltpu.VMEM)] * len(arrays),
        out_specs=[pl.BlockSpec(memory_space=pl.ANY)] * len(arrays),
        scratch_shapes=[pltpu.SemaphoreType.DMA((len(arrays), PIECES))],
    )(*arrays)


def on_device_fused(q, k, v, g, w, a, b):
    rows, feats = q.shape
    cols = g.shape[1]
    rank = b.shape[0]
    tokens, window = BLOCKS * rows, 2 * BLOCKS * rows
    vmem, hbm = pl.BlockSpec(memory_space=pltpu.VMEM), pl.BlockSpec(memory_space=pl.ANY)
    scratch = [
        ((tokens, 2 * HD), BF16), ((window, 2 * HD), BF16), ((window, 2 * HD), BF16), ((tokens, 2 * HD), BF16),
        ((tokens, HD), BF16), ((window, HD), BF16), ((window, HD), BF16), ((tokens, HD), BF16),
        ((rank, feats), BF16), (b.shape, BF16), ((2 * rows, cols), BF16), (w.shape, BF16), ((rows, cols), BF16), ((2 * rows, feats), F32),
        ((rows, feats), BF16), ((rows, feats), BF16), ((CUTS, rank, 2 * rows // CUTS), F32), ((CUTS, rank, 2 * rows // CUTS), F32),
        ((2 * rows // CUTS, rank), F32), ((2, rank, tokens), BF16), ((rows, feats), BF16),
        ((3, HD, window), BF16), ((3, HD, window), BF16), ((3, window, tokens), BF16), ((3, HD, tokens), F32),
        ((3, HD, tokens), F32), ((6, window, HD), F32), ((8, tokens), F32), ((8, tokens), F32), ((8, tokens), F32), ((8, tokens), F32),
        ((6, tokens, HD), BF16), ((6, tokens, HD), BF16), ((9, tokens, HD), BF16), ((3, tokens, HD), F32),
        ((BLOCKS, rows, HD), BF16), ((BLOCKS, rows, HD), BF16), ((BLOCKS, rows, HD), BF16),
        ((2 * rank + 8, tokens), F32), ((BLOCKS, 2 * rank + 8, rows), F32), ((BLOCKS, rank + 8, rows), F32), ((rank, rows), F32), ((rank, rows), F32),
        ((2, rank, cols // 2), F32), ((rank, cols // 2), F32), ((2 * BLOCKS, rank, HD), F32),
        ((2, rank, cols // 2), F32), ((rank, 2 * HD), F32), ((rank, 2 * HD), F32), ((2 * BLOCKS, rank, 2 * HD), F32),
    ]
    dq, dk, dv, down, up = pl.pallas_call(
        fused_kernel,
        out_shape=(
            jax.ShapeDtypeStruct((rows, feats), BF16),
            jax.ShapeDtypeStruct((rows, feats), BF16),
            jax.ShapeDtypeStruct((rows, feats), BF16),
            jax.ShapeDtypeStruct((rank, feats), F32),
            jax.ShapeDtypeStruct((rank, cols), F32),
        ),
        in_specs=[hbm] * 7,
        out_specs=[vmem] * 5,
        scratch_shapes=[pltpu.VMEM(shape, kind) for shape, kind in scratch]
        + [pltpu.SemaphoreType.DMA((SENDS,)), pltpu.SemaphoreType.DMA((RECEIVES,))],
        compiler_params=pltpu.CompilerParams(
            collective_id=0, has_side_effects=True, vmem_limit_bytes=60 * 1024 * 1024
        ),
    )(q, k, v, g, w, a.T, b)
    dq, dk, dv, down, up = written(dq, dk, dv, down, up)
    return dq, dk, dv, down.T, up


def one_group(mesh, rows, feats, width):
    seq, head, sub = mesh.shape["seq"], mesh.shape["head"], mesh.shape["sub"]
    return (
        sub == 2
        and head == 2
        and rows == HD
        and seq == 2 * BLOCKS
        and seq * sub * rows == GROUP
        and feats == seq * HD
        and width == 2 * seq * HD
    )


def solution(mesh):
    in_specs = (
        P(("rep", "seq", "sub"), "head"),
        P(("rep", "seq", "sub"), "head"),
        P(("rep", "seq", "sub"), "head"),
        P(("rep", "seq", "sub"), "head"),
        P("head", "sub"),
        P("head", None),
        P(),
    )
    out_specs = (
        P(("rep", "seq", "sub"), "head"),
        P(("rep", "seq", "sub"), "head"),
        P(("rep", "seq", "sub"), "head"),
        P(("rep", "head"), None),
        P("rep", "head"),
    )

    def on_device(*local):
        if one_group(mesh, *local[0].shape, local[3].shape[1]):
            return on_device_fused(*local)
        return on_device_windows(*local)

    return jax.shard_map(
        on_device, mesh=mesh, in_specs=in_specs, out_specs=out_specs, check_vma=False
    )
```

```python
import jax
import jax.numpy as jnp
from jax import lax
from jax.experimental import pallas as pl
from jax.experimental.pallas import tpu as pltpu
from jax.sharding import PartitionSpec as P

HD = 128
GROUP = 2048


def passed_along(value, axis, by):
    peers = lax.axis_size(axis)
    return lax.ppermute(value, axis, [(i, (i + by) % peers) for i in range(peers)])


def placed_visible(row_count, window_rows, seq_total, first_row, back_rows, roll_by):
    query_pos = first_row + lax.broadcasted_iota(jnp.int32, (row_count, window_rows), 0)
    key_pos = (
        first_row
        - back_rows
        + seq_total
        + lax.broadcasted_iota(jnp.int32, (row_count, window_rows), 1)
    ) % seq_total
    query_order = (query_pos - roll_by + seq_total) % seq_total
    key_order = (key_pos - roll_by + seq_total) % seq_total
    return (query_order // GROUP == key_order // GROUP) & (key_order <= query_order)


def softmax_rows(query_head, keys_head, visible):
    scores = lax.dot_general(
        query_head, keys_head, (((1,), (1,)), ((), ())), preferred_element_type=jnp.float32
    )
    scores = jnp.where(visible, scores * HD ** (-0.5), -jnp.inf)
    highest = jnp.max(scores, axis=1, keepdims=True)
    powers = jnp.exp(scores - highest)
    return powers / jnp.sum(powers, axis=1, keepdims=True)


def head_forward(query_head, window_head, visible):
    prob = softmax_rows(query_head, window_head[0], visible)
    return jnp.dot(
        prob.astype(jnp.bfloat16), window_head[1], preferred_element_type=jnp.float32
    ).astype(jnp.bfloat16)


def head_backward(query_head, window_head, dout_head, visible):
    prob = softmax_rows(query_head, window_head[0], visible)
    prob_lo = prob.astype(jnp.bfloat16)
    dprob = lax.dot_general(
        dout_head, window_head[1], (((1,), (1,)), ((), ())), preferred_element_type=jnp.float32
    )
    delta = jnp.sum(prob * dprob, axis=1, keepdims=True)
    dscore = (prob * (dprob - delta) * HD ** (-0.5)).astype(jnp.bfloat16)
    grad_q = jnp.dot(dscore, window_head[0], preferred_element_type=jnp.float32).astype(
        jnp.bfloat16
    )
    grad_k = lax.dot_general(
        dscore, query_head, (((0,), (0,)), ((), ())), preferred_element_type=jnp.float32
    )
    grad_v = lax.dot_general(
        prob_lo, dout_head, (((0,), (0,)), ((), ())), preferred_element_type=jnp.float32
    )
    return (grad_q, jnp.stack((grad_k.astype(jnp.bfloat16), grad_v.astype(jnp.bfloat16))))


def attend_window(query_rows, window, dout_rows, visible):
    row_count, feat_count = query_rows.shape
    heads_here = feat_count // HD
    window_rows = window.shape[1]
    window_heads = window.reshape(2, window_rows, heads_here, HD).transpose(2, 0, 1, 3)
    query_heads = query_rows.reshape(row_count, heads_here, HD).transpose(1, 0, 2)
    dout_heads = dout_rows.reshape(row_count, heads_here, HD).transpose(1, 0, 2)
    attn_heads = lax.map(
        lambda pieces: head_forward(pieces[0], pieces[1], visible), (query_heads, window_heads)
    )
    grad_q_heads, pair_heads = lax.map(
        lambda pieces: head_backward(pieces[0], pieces[1], pieces[2], visible),
        (query_heads, window_heads, dout_heads),
    )
    attention_output = attn_heads.transpose(1, 0, 2).reshape(row_count, feat_count)
    query_gradient = grad_q_heads.transpose(1, 0, 2).reshape(row_count, feat_count)
    pair_grads = pair_heads.transpose(1, 2, 0, 3).reshape(2, window_rows, feat_count)
    return (attention_output, query_gradient, pair_grads)


def on_device_windows(
    head_query_rows,
    head_key_rows,
    head_value_rows,
    output_gradient,
    output_matrix,
    adapter_down_weight,
    adapter_up_weight,
):
    tokens_dev, feat_dev = head_query_rows.shape
    head_index = lax.axis_index("head")
    shifted = head_index >= lax.axis_size("head") // 2
    total_gradient = lax.all_gather(output_gradient, "head", axis=1, tiled=True)
    projected_output = lax.dot_general(
        total_gradient,
        lax.all_gather(output_matrix, "sub", axis=1, tiled=True),
        (((1,), (1,)), ((), ())),
        preferred_element_type=jnp.float32,
    )
    adapter_upward = lax.dot_general(
        total_gradient,
        adapter_up_weight,
        (((1,), (1,)), ((), ())),
        preferred_element_type=jnp.float32,
    )
    adapter_backward = jnp.dot(
        adapter_upward, adapter_down_weight.astype(jnp.float32).T, precision=lax.Precision.HIGHEST
    )
    attention_gradient = (projected_output + 2.0 * adapter_backward).astype(jnp.bfloat16)
    sub_count = lax.axis_size("sub")
    block_rows = tokens_dev * sub_count
    seq_total = block_rows * lax.axis_size("seq")
    reach = max(GROUP // block_rows - 1, 1)
    roll_by = jnp.where(shifted, GROUP // 2, 0)
    stacked = jnp.stack((head_query_rows, head_key_rows, head_value_rows, attention_gradient))
    moved = lax.all_to_all(stacked, "sub", split_axis=2, concat_axis=1, tiled=True)
    own_pair = moved[1:3]
    received = [passed_along(own_pair, "seq", distance) for distance in range(reach, 0, -1)]
    window = jnp.concatenate(received + [own_pair], axis=1)
    first_row = lax.axis_index("seq") * block_rows
    visible = placed_visible(
        block_rows, window.shape[1], seq_total, first_row, reach * block_rows, roll_by
    )
    attn_local, grad_q_local, pair_grads = attend_window(moved[0], window, moved[3], visible)
    running = pair_grads[:, reach * block_rows :].astype(jnp.float32)
    for distance in range(1, reach + 1):
        begin_row = (reach - distance) * block_rows
        block_terms = pair_grads[:, begin_row : begin_row + block_rows]
        returned = passed_along(block_terms, "seq", -distance)
        running = running + returned.astype(jnp.float32)
    pair_local = running.astype(jnp.bfloat16)
    back = jnp.stack((attn_local, grad_q_local, pair_local[0], pair_local[1]))
    restored = lax.all_to_all(back, "sub", split_axis=1, concat_axis=2, tiled=True)
    attention_output = restored[0]
    query_gradient = restored[1]
    key_gradient = restored[2]
    value_gradient = restored[3]
    middle_piece = jnp.dot(
        attention_output, adapter_down_weight, preferred_element_type=jnp.float32
    )
    down_gradient_part = 2.0 * jnp.dot(
        attention_output.astype(jnp.float32).T, adapter_upward, precision=lax.Precision.HIGHEST
    )
    adapter_middle = lax.psum(middle_piece, "head")
    up_gradient_part = 2.0 * jnp.dot(
        adapter_middle.T, output_gradient.astype(jnp.float32), precision=lax.Precision.HIGHEST
    )
    adapter_down_gradient, adapter_up_gradient = lax.psum(
        (down_gradient_part, up_gradient_part), ("seq", "sub")
    )
    return (
        query_gradient,
        key_gradient,
        value_gradient,
        adapter_down_gradient,
        adapter_up_gradient,
    )


SCALE = HD ** (-0.5)
F32, BF16 = jnp.float32, jnp.bfloat16


def dot_nn(left, right):
    return lax.dot_general(left, right, (((1,), (0,)), ((), ())), preferred_element_type=F32)


def dot_nt(left, right):
    return lax.dot_general(left, right, (((1,), (1,)), ((), ())), preferred_element_type=F32)


MESH = pl.DeviceIdType.MESH
BLOCKS = 4
CUTS = 2
PIECES = 1
LOG2E = 1.4426950408889634
NONE = -1e30


NAMES = (
    "big0", "big1", "kv", "q", "kvx", "qx", "kvp", "kvxp", "g", "gx", "w", "a", "b", "gl", "part0",
    "part1", "lora0", "lora1", "up", "stat", "share", "theirs0", "theirs1", "theirs2", "home",
    "home2", "far", "far2", "mid", "midx", "us", "uy", "ur", "uh", "ds", "dn",
)
PLACES = {name: place for place, name in enumerate(NAMES)}
GROUPS = 8
TALLY, BLOCK_BYTES = 1024, 4096


def combine(mine, other):
    top = jnp.maximum(mine[0], other[0])
    c = SCALE * LOG2E
    e1, e2 = jnp.exp2((mine[0] - top) * c), jnp.exp2((other[0] - top) * c)
    w = 1.0 / (mine[1] * e1 + other[1] * e2)
    return e1 * w, e2 * w


def fused_kernel(
    q_ref, k_ref, v_ref, g_ref, w_ref, a_hbm, b_hbm,
    dq_out, dk_out, dv_out, down_out, up_out,
    qb, kb, vb, gb, qr, kr, vr, gr,
    a_ref, b_ref, big, wb, gl, xb, xs, xr, ls, lr, lt, lub, dob,
    kt, vt, probs, ot, gt, acc, stat_s, stat_r, share_s, share_r, ts, tr, hs, dqs,
    rk, rv, rq, ms, mb, mf, mxs, mxr, us, usr, ys, yr, zo, uf, dss, dsr, dnr,
    tally, ssem, rsem,
):
    s, x, c = lax.axis_index("seq"), lax.axis_index("head"), lax.axis_index("sub")
    n = BLOCKS
    half, j = s // n, lax.rem(s, n)
    late = lax.rem(half + x, 2) == 1
    early = lax.rem(half + x, 2) == 0
    partner = {"sub": 1 - c}
    p = PLACES
    held = {"always": None, "late": late, "early": early, "other": c != x}
    groups = []

    def at(base, many):
        return pl.ds(pl.multiple_of(base, many), many)

    def send(src, dst, place, to, when="always"):
        size = src.dtype.itemsize
        for extent in src.shape:
            size *= extent
        for group in groups:
            if group[0] == when and group[1] + size <= TALLY * BLOCK_BYTES:
                break
        else:
            group = [when, 0]
            groups.append(group)
        group[1] += size
        copy = pltpu.make_async_remote_copy(
            src_ref=src, dst_ref=dst, send_sem=ssem.at[groups.index(group)], recv_sem=rsem.at[p[place]],
            device_id=to, device_id_type=MESH,
        )
        if held[when] is None:
            copy.start()
        else:
            pl.when(held[when])(copy.start)

    def all_sent():
        for i, (when, size) in enumerate(groups):
            sent = tally.at[pl.ds(0, size // BLOCK_BYTES)]
            copy = pltpu.make_async_remote_copy(
                src_ref=sent, dst_ref=sent, send_sem=ssem.at[i], recv_sem=rsem.at[0],
                device_id=partner, device_id_type=MESH,
            )
            if held[when] is None:
                copy.wait_send()
            else:
                pl.when(held[when])(copy.wait_send)

    def got(ref, place):
        pltpu.make_async_remote_copy(
            src_ref=ref, dst_ref=ref, send_sem=ssem.at[0], recv_sem=rsem.at[p[place]],
            device_id=partner, device_id_type=MESH,
        ).wait_recv()

    def local(src, dst, place):
        copy = pltpu.make_async_copy(src, dst, rsem.at[p[place]])
        copy.start()
        return copy

    def near(d):
        o = lax.rem(j + d, n)
        return o, {"seq": half * n + o}

    def far(d):
        o = lax.rem(j + d, n)
        return o, {"seq": (1 - half) * n + o}

    barrier = pltpu.get_barrier_semaphore()
    greeted = [near(d)[1] for d in range(1, n)] + [far(d)[1] for d in range(n)]
    pair_s = s + 1 - 2 * lax.rem(s, 2)
    greeted += [{"seq": pair_s, "sub": 1 - c}, partner, {"head": 1 - x}, {"head": 1 - x, "sub": 1 - c}]
    for device in greeted:
        pl.semaphore_signal(barrier, inc=1, device_id=device, device_id_type=MESH)
    pl.semaphore_wait(barrier, len(greeted))

    part_rows = HD // CUTS
    for r in range(CUTS):
        mine_g = at(r * 2 * part_rows + c * part_rows, part_rows)
        from_g = g_ref.at[pl.ds(r * part_rows, part_rows)]
        place = f"big{r}"
        send(from_g, big.at[mine_g], place, {"head": 1 - x, "sub": x})
        send(from_g, big.at[mine_g], place, partner, when="other")

        @pl.when(c == x)
        def _():
            local(from_g, big.at[mine_g], place)

    w_copy = local(w_ref, wb, "w")
    low_rank_copies = [local(a_hbm, a_ref, "a"), local(b_hbm, b_ref, "b")]
    mine_k, mine_q = at(j * 2 * HD + c * HD, HD), at(j * HD, HD)
    own = at(j * 2 * HD, 2 * HD)
    for d in range(1, n):
        o, to = near(d)
        cols = at(o * 2 * HD, 2 * HD)
        send(k_ref.at[:, cols], kb.at[mine_k], "kv", to)
        send(v_ref.at[:, cols], vb.at[mine_k], "kv", to)
        send(q_ref.at[:, cols], qb.at[mine_q], "q", to)
    for d in range(n):
        o, to = far(d)
        first, second = at(o * 2 * HD, HD), at(o * 2 * HD + HD, HD)
        send(k_ref.at[:, first], kr.at[mine_k], "kvx", to, when="early")
        send(v_ref.at[:, first], vr.at[mine_k], "kvx", to, when="early")
        send(q_ref.at[:, second], qr.at[mine_q], "qx", to, when="late")
    local(k_ref.at[:, own], kb.at[mine_k], "kv")
    local(v_ref.at[:, own], vb.at[mine_k], "kv")
    local(q_ref.at[:, own], qb.at[mine_q], "q")
    send(k_ref.at[:, own], kb.at[mine_k], "kvp", partner)
    send(v_ref.at[:, own], vb.at[mine_k], "kvp", partner)
    gl_copy = local(g_ref, gl, "gl")

    w_copy.wait()
    for copy in low_rank_copies:
        copy.wait()
    feats, cols_dev, width = wb.shape[0], big.shape[1], 2 * HD
    ups = []

    def project_cut(r):
        both = pl.ds(r * 2 * part_rows, 2 * part_rows)
        got(big.at[both], f"big{r}")

        def project(f, carry):
            piece = at(f * width, width)
            xb[both, piece] = dot_nt(big[both, :], wb[piece, :])
            return carry

        ls[r] = dot_nt(b_ref[:, at(c * cols_dev, cols_dev)], big[both, :])
        send(ls.at[r], lr.at[r], f"lora{r}", partner)
        lax.fori_loop(0, feats // width, project, 0)
        span = pl.ds(r * part_rows, part_rows)
        xs[span, :] = xb[at((2 * r + 1 - c) * part_rows, part_rows), :].astype(BF16)
        send(xs.at[span], xr.at[span], f"part{r}", partner)

    def gradient_cut(r):
        span = pl.ds(r * part_rows, part_rows)
        got(lr.at[r], f"lora{r}")
        up_r = ls[r] + lr[r]
        lt[...] = (2.0 * up_r).T
        ups.append(up_r)
        lora = dot_nn(lt[at(c * part_rows, part_rows), :].astype(BF16), a_ref[...])
        got(xr.at[span], f"part{r}")
        own_x = xb[at((2 * r + c) * part_rows, part_rows), :]
        dob[span, :] = (own_x + xr[span, :].astype(F32) + lora).astype(BF16)
        mine_d = at(j * HD + r * part_rows, part_rows)
        for d in range(1, n):
            o, to = near(d)
            send(dob.at[span, at(o * 2 * HD, 2 * HD)], gb.at[mine_d], "g", to)
        for d in range(n):
            o, to = far(d)
            send(dob.at[span, at(o * 2 * HD + HD, HD)], gr.at[mine_d], "gx", to, when="late")

    for r in range(CUTS - 1):
        project_cut(r)
        gradient_cut(r)
    project_cut(CUTS - 1)
    got(kb, "kv")
    for d in range(1, n):
        o = lax.rem(j + d, n)
        block = at(o * 2 * HD + c * HD, HD)
        send(kb.at[block], kb.at[block], "kvp", partner)
        send(vb.at[block], vb.at[block], "kvp", partner)

    gradient_cut(CUTS - 1)
    gb[mine_q, :] = dob[:, own]
    up_mine = jnp.where(
        c == 0,
        jnp.concatenate([u[:, :part_rows] for u in ups], axis=1),
        jnp.concatenate([u[:, part_rows:] for u in ups], axis=1),
    )
    here = lub.at[half, :, at(j * HD, HD)]
    lub[half, :, at(j * HD, HD)] = up_mine.astype(BF16)
    for d in range(1, n):
        o, to = near(d)
        send(here, here, "up", to)
    for d in range(n):
        o, to = far(d)
        send(here, here, "up", to)

    @pl.when(late)
    def _():
        got(kr, "kvx")

    for o in range(n):
        block = at(o * 2 * HD + c * HD, HD)
        send(kr.at[block], kr.at[block], "kvxp", partner, when="late")
        send(vr.at[block], vr.at[block], "kvxp", partner, when="late")
    got(qb, "q")
    got(kb, "kvp")

    @pl.when(late)
    def _():
        got(kr, "kvxp")
        qr[...] = qb[:, :HD]

    @pl.when(early)
    def _():
        got(qr, "qx")
        kr[...] = kb[:, HD:]
        vr[...] = vb[:, HD:]

    tile = 2 * HD
    total = kb.shape[0]
    lanes = (slice(0, HD), slice(HD, 2 * HD), slice(0, HD))
    keys, values = (kb, kb, kr), (vb, vb, vr)
    queries, douts = (qb, qb, qr), (gb, gb, gr)
    key_at = lax.broadcasted_iota(jnp.int32, (2 * tile, tile), 0)
    row = lax.broadcasted_iota(jnp.int32, (2 * tile, tile), 1)
    seen = key_at <= row + jnp.where(row >= HD, HD, 0) + c * HD

    def extent(part, u):
        return total if part == 2 else (u + 1) * 2 * tile

    tops, sums = [], []
    for part in range(3):
        kt[part] = keys[part][:, lanes[part]].T
        vt[part] = values[part][:, lanes[part]].T
        queries_t = queries[part][:, lanes[part]].T
        top_u, sum_u = [], []
        for u in range(2):
            ext = extent(part, u)
            q_t = queries_t[:, u * tile : (u + 1) * tile]
            scores = dot_nn(keys[part][:ext, lanes[part]], q_t)
            if part < 2:
                settled = ext - 2 * tile
                edge = jnp.where(seen, scores[settled:, :], NONE)
                scores = edge if settled == 0 else jnp.concatenate((scores[:settled, :], edge), axis=0)
            top = jnp.max(scores, axis=0, keepdims=True)
            powers = jnp.exp2((scores - top) * (SCALE * LOG2E))
            top_u.append(top)
            sum_u.append(jnp.sum(powers, axis=0, keepdims=True))
            low = powers.astype(BF16)
            probs[part, :ext, u * tile : (u + 1) * tile] = low
            ot[part, :, u * tile : (u + 1) * tile] = dot_nn(vt[part, :, :ext], low)
        tops.append(jnp.concatenate(top_u, axis=1))
        sums.append(jnp.concatenate(sum_u, axis=1))

    local_stats = [(tops[part], sums[part]) for part in range(3)]
    for r in range(2):
        stat_s[r : r + 1, :] = jnp.where(late, local_stats[1][r], local_stats[2][r])
    nothing = (NONE, 0.0)
    other_0 = tuple(jnp.where(late, local_stats[2][r], nothing[r]) for r in range(2))
    first, second = combine(local_stats[0], other_0)
    attn_0 = (ot[0] * first + jnp.where(late, ot[2] * second, 0.0)).astype(BF16)
    down = [a_ref[:, at(j * 2 * HD + i * HD, HD)] for i in range(2)]
    alone = ot[1] * jnp.where(late, 1.0, 1.0 / sums[1])
    mid_0, mid_1 = dot_nn(down[0], attn_0), dot_nn(down[1], alone.astype(BF16))
    rank = mid_0.shape[0]
    ms[:rank, :] = mid_0 + jnp.where(late, 0.0, mid_1)
    ms[rank : 2 * rank, :] = jnp.where(late, mid_1, dot_nn(down[1], ot[2].astype(BF16)))
    ms[2 * rank :, :] = stat_s[...]
    for d in range(1, n):
        o, to = near(d)
        send(ms.at[:, at(o * HD, HD)], mb.at[j], "mid", to)
    for d in range(n):
        o, to = far(d)
        send(ms.at[pl.ds(rank, rank + 8), at(o * HD, HD)], mf.at[j], "far", to, when="early")
    mb[j] = ms[:, at(j * HD, HD)]
    send(stat_s, stat_r, "stat", {"seq": (1 - half) * n + j})

    def backward(part, w, delta):
        delta = delta * w
        for u in reversed(range(2)):
            ext = extent(part, u)
            span = slice(u * tile, (u + 1) * tile)
            g_t = gt[part, :, span] * w[:, span]
            g = g_t.T.astype(BF16)
            low = probs[part, :ext, span]
            dprob = dot_nn(values[part][:ext, lanes[part]], g_t.astype(BF16))
            dscore = (dprob - delta[:, span]).astype(BF16) * low
            dq_t = dot_nn(kt[part, :, :ext], dscore)
            dq = (dq_t * SCALE).T
            dk = dot_nn(dscore, queries[part][span, lanes[part]])
            dv = dot_nn(low, g)
            at_k, at_v = 2 * part, 2 * part + 1
            if u == 1:
                acc[at_k], acc[at_v] = dk, dv
            else:
                acc[at_k, :ext, :] += dk
                acc[at_v, :ext, :] += dv
            dqs[part, span, :] = dq

    def to_partner(part, when="always"):
        for t, scale in ((2 * part, SCALE), (2 * part + 1, 1.0)):
            for o in range(n):
                block = acc[t, at(o * 2 * HD + (1 - c) * HD, HD), :]
                ts[t, pl.ds(o * HD, HD), :] = (block * scale).astype(BF16)
        both = pl.ds(2 * part, 2)
        send(ts.at[both], tr.at[both], f"theirs{part}", partner, when=when)

    def add_theirs(part):
        got(tr.at[pl.ds(2 * part, 2)], f"theirs{part}")
        for t, scale in ((2 * part, SCALE), (2 * part + 1, 1.0)):
            for o in range(n):
                span = pl.ds(o * HD, HD)
                block = acc[t, at(o * 2 * HD + c * HD, HD), :]
                hs[t, span, :] = (block * scale + tr[t, span, :].astype(F32)).astype(BF16)

    def home_sends(part, t, out):
        cols = at(j * 2 * HD + part * HD, HD)
        for d in range(1, n):
            o, to = near(d)
            send(hs.at[t, at(o * HD, HD)], out.at[:, cols], "home", to)
        out[:, cols] = hs[t, mine_q, :]

    def pair_home(part):
        add_theirs(part)
        home_sends(part, 2 * part, dk_out)
        home_sends(part, 2 * part + 1, dv_out)

    got(gb.at[pl.ds(0, (n - 1) * HD)], "g")

    @pl.when(late)
    def _():
        gr[...] = gb[:, :HD]

    @pl.when(early)
    def _():
        got(gr, "gx")

    shares = []
    for part in range(3):
        g_t = douts[part][:, lanes[part]].astype(F32).T
        gt[part] = g_t
        shares.append(jnp.sum(ot[part] * g_t, axis=0, keepdims=True))
    share_s[...] = jnp.broadcast_to(jnp.where(late, shares[1], shares[2]), share_s.shape)
    send(share_s, share_r, "share", {"seq": (1 - half) * n + j})
    backward(0, first, first * shares[0] + second * jnp.where(late, shares[2], 0.0))
    to_partner(0)
    got(mb.at[pl.ds(0, n - 1)], "mid")
    mid = mb[0, :rank, :]
    for o in range(1, n):
        mid = mid + mb[o, :rank, :]
    mxs[...] = mid

    @pl.when(late)
    def _():
        got(mf, "far")
        whole = mxs[...]
        for o in range(n):
            near_stat = (mb[o, 2 * rank : 2 * rank + 1, :], mb[o, 2 * rank + 1 : 2 * rank + 2, :])
            far_stat = (mf[o, rank : rank + 1, :], mf[o, rank + 1 : rank + 2, :])
            w_near, w_far = combine(near_stat, far_stat)
            whole = whole + mb[o, rank : 2 * rank, :] * w_near + mf[o, :rank, :] * w_far
        mxs[...] = whole

    send(mxs, mxr, "midx", {"head": 1 - x})
    pair_home(0)
    gl_copy.wait()
    got(mxr, "midx")
    mid = (2.0 * (mxs[...] + mxr[...])).astype(BF16)
    up = dot_nn(mid, gl[...])
    side = us.shape[2]
    us[0], us[1] = up[:, :side], up[:, side:]
    send(us.at[1 - c], usr, "us", partner)
    got(stat_r, "stat")
    remote = (stat_r[0:1, :], stat_r[1:2, :])
    other_1 = tuple(jnp.where(late, remote[r], nothing[r]) for r in range(2))
    other_2 = tuple(jnp.where(late, local_stats[0][r], remote[r]) for r in range(2))
    w_1, w_2 = combine(local_stats[1], other_1), combine(local_stats[2], other_2)
    attn_1 = (ot[1] * w_1[0]).astype(BF16)
    attn_2 = (ot[2] * w_2[0]).astype(BF16)
    got(b_ref.at[:, pl.ds(0, (2 * n - 1) * HD)], "up")
    near_up = lub[half]
    dss[:, :HD] = dot_nt(near_up, attn_0)
    dss[:, HD:] = dot_nt(near_up, attn_1) + jnp.where(late, 0.0, dot_nt(lub[1 - half], attn_2))
    send(dss, dsr, "ds", partner)
    got(share_r, "share")
    far_share = share_r[0:1, :]
    backward(2, w_2[0], w_2[0] * shares[2] + w_2[1] * jnp.where(late, shares[0], far_share))
    got(dsr, "ds")
    dnr[s] = (2.0 * (dss[...] + dsr[...])).astype(BF16)
    for d in range(1, 2 * n):
        other = lax.rem(s + d, 2 * n)
        send(dnr.at[s], dnr.at[s], "dn", {"seq": other})
    got(usr, "us")
    us[c] += usr[...]
    quarter, mine_y = side // 2, lax.rem(s, 2)
    ys[...] = us[c, :, at((1 - mine_y) * quarter, quarter)].astype(BF16)
    send(ys, yr, "uy", {"seq": pair_s})
    to_partner(2, when="late")
    hs[6] = (dqs[0] + jnp.where(late, dqs[2], 0.0)).astype(BF16)
    home_sends(0, 6, dq_out)

    @pl.when(early)
    def _():
        hs[8] = dqs[2].astype(BF16)

    for d in range(n):
        o, to = far(d)
        send(hs.at[8, at(o * HD, HD)], rq.at[j], "far2", to, when="early")
    backward(1, w_1[0], w_1[0] * shares[1] + w_1[1] * jnp.where(late, far_share, 0.0))
    for t in (0, 1):
        acc[2 + t] += jnp.where(early, acc[4 + t], 0.0)
    to_partner(1)
    hs[7] = dqs[1].astype(BF16)
    home_sends(1, 7, dq_out)
    got(yr, "uy")
    level = s // 2
    zo[level] = (us[c, :, at(mine_y * quarter, quarter)] + yr[...].astype(F32)).astype(BF16)
    for d in range(1, n):
        send(zo.at[level], zo.at[level], "ur", {"seq": lax.rem(s + 2 * d, 2 * n)})

    @pl.when(late)
    def _():
        add_theirs(2)

    for t, to_ref in ((4, rk), (5, rv)):
        for d in range(n):
            o, to = far(d)
            send(hs.at[t, at(o * HD, HD)], to_ref.at[j], "home2", to, when="late")
    pair_home(1)
    got(dnr.at[pl.ds(0, 2 * n - 1)], "dn")
    for i in range(n):
        down_out[:, i * 2 * HD : (i + 1) * 2 * HD] = dnr[i].astype(F32) + dnr[i + n].astype(F32)
    got(zo.at[pl.ds(0, n - 1)], "ur")
    total_up = zo[0].astype(F32)
    for i in range(1, n):
        total_up = total_up + zo[i].astype(F32)
    mine = at(c * side + mine_y * quarter, quarter)
    uf[:, mine] = total_up
    for to in ({"seq": pair_s}, partner, {"seq": pair_s, "sub": 1 - c}):
        send(uf.at[:, mine], uf.at[:, mine], "uh", to)

    blocks = 6 * (n - 1) * HD * HD // probs.shape[2]
    got(probs.at[0, pl.ds(0, blocks)], "home")

    @pl.when(late)
    def _():
        got(rq, "far2")
        for o in range(n):
            cols = slice(o * 2 * HD + HD, (o + 1) * 2 * HD)
            dq_out[:, cols] = (dq_out[:, cols].astype(F32) + rq[o].astype(F32)).astype(BF16)

    @pl.when(early)
    def _():
        got(kr, "home2")
        for out, ref in ((dk_out, rk), (dv_out, rv)):
            for o in range(n):
                cols = slice(o * 2 * HD, o * 2 * HD + HD)
                out[:, cols] = (out[:, cols].astype(F32) + ref[o].astype(F32)).astype(BF16)

    got(uf.at[:, pl.ds(0, 3 * quarter)], "uh")
    up_out[...] = uf[...]
    all_sent()


def written(*arrays):
    def kernel(*refs):
        copies = []
        for i, array in enumerate(arrays):
            rows = array.shape[0] // PIECES
            for k in range(PIECES):
                piece = pl.ds(k * rows, rows)
                copies.append(
                    pltpu.make_async_copy(
                        refs[i].at[piece], refs[len(arrays) + i].at[piece], refs[-1].at[i, k]
                    )
                )
        for copy in copies:
            copy.start()
        for copy in copies:
            copy.wait()

    return pl.pallas_call(
        kernel,
        out_shape=tuple(jax.ShapeDtypeStruct(array.shape, array.dtype) for array in arrays),
        in_specs=[pl.BlockSpec(memory_space=pltpu.VMEM)] * len(arrays),
        out_specs=[pl.BlockSpec(memory_space=pl.ANY)] * len(arrays),
        scratch_shapes=[pltpu.SemaphoreType.DMA((len(arrays), PIECES))],
    )(*arrays)


def on_device_fused(q, k, v, g, w, a, b):
    rows, feats = q.shape
    cols = g.shape[1]
    rank = b.shape[0]
    tokens, window = BLOCKS * rows, 2 * BLOCKS * rows
    vmem, hbm = pl.BlockSpec(memory_space=pltpu.VMEM), pl.BlockSpec(memory_space=pl.ANY)
    scratch = [
        ((tokens, 2 * HD), BF16), ((window, 2 * HD), BF16), ((window, 2 * HD), BF16), ((tokens, 2 * HD), BF16),
        ((tokens, HD), BF16), ((window, HD), BF16), ((window, HD), BF16), ((tokens, HD), BF16),
        ((rank, feats), BF16), (b.shape, BF16), ((2 * rows, cols), BF16), (w.shape, BF16), ((rows, cols), BF16), ((2 * rows, feats), F32),
        ((rows, feats), BF16), ((rows, feats), BF16), ((CUTS, rank, 2 * rows // CUTS), F32), ((CUTS, rank, 2 * rows // CUTS), F32),
        ((2 * rows // CUTS, rank), F32), ((2, rank, tokens), BF16), ((rows, feats), BF16),
        ((3, HD, window), BF16), ((3, HD, window), BF16), ((3, window, tokens), BF16), ((3, HD, tokens), F32),
        ((3, HD, tokens), F32), ((6, window, HD), F32), ((8, tokens), F32), ((8, tokens), F32), ((8, tokens), F32), ((8, tokens), F32),
        ((6, tokens, HD), BF16), ((6, tokens, HD), BF16), ((9, tokens, HD), BF16), ((3, tokens, HD), F32),
        ((BLOCKS, rows, HD), BF16), ((BLOCKS, rows, HD), BF16), ((BLOCKS, rows, HD), BF16),
        ((2 * rank + 8, tokens), F32), ((BLOCKS, 2 * rank + 8, rows), F32), ((BLOCKS, rank + 8, rows), F32), ((rank, rows), F32), ((rank, rows), F32),
        ((2, rank, cols // 2), F32), ((rank, cols // 2), F32), ((rank, cols // 4), BF16), ((rank, cols // 4), BF16),
        ((BLOCKS, rank, cols // 4), BF16), ((rank, cols), F32), ((rank, 2 * HD), F32), ((rank, 2 * HD), F32), ((2 * BLOCKS, rank, 2 * HD), BF16),
        ((TALLY, 8, HD), F32),
    ]
    dq, dk, dv, down, up = pl.pallas_call(
        fused_kernel,
        out_shape=(
            jax.ShapeDtypeStruct((rows, feats), BF16),
            jax.ShapeDtypeStruct((rows, feats), BF16),
            jax.ShapeDtypeStruct((rows, feats), BF16),
            jax.ShapeDtypeStruct((rank, feats), F32),
            jax.ShapeDtypeStruct((rank, cols), F32),
        ),
        in_specs=[hbm] * 7,
        out_specs=[vmem] * 5,
        scratch_shapes=[pltpu.VMEM(shape, kind) for shape, kind in scratch]
        + [pltpu.SemaphoreType.DMA((GROUPS,)), pltpu.SemaphoreType.DMA((len(PLACES),))],
        compiler_params=pltpu.CompilerParams(
            collective_id=0, has_side_effects=True, vmem_limit_bytes=60 * 1024 * 1024
        ),
    )(q, k, v, g, w, a.T, b)
    dq, dk, dv, down, up = written(dq, dk, dv, down, up)
    return dq, dk, dv, down.T, up


def one_group(mesh, rows, feats, width):
    seq, head, sub = mesh.shape["seq"], mesh.shape["head"], mesh.shape["sub"]
    return (
        sub == 2
        and head == 2
        and rows == HD
        and seq == 2 * BLOCKS
        and seq * sub * rows == GROUP
        and feats == seq * HD
        and width == 2 * seq * HD
    )


def solution(mesh):
    in_specs = (
        P(("rep", "seq", "sub"), "head"),
        P(("rep", "seq", "sub"), "head"),
        P(("rep", "seq", "sub"), "head"),
        P(("rep", "seq", "sub"), "head"),
        P("head", "sub"),
        P("head", None),
        P(),
    )
    out_specs = (
        P(("rep", "seq", "sub"), "head"),
        P(("rep", "seq", "sub"), "head"),
        P(("rep", "seq", "sub"), "head"),
        P(("rep", "head"), None),
        P("rep", "head"),
    )

    def on_device(*local):
        if one_group(mesh, *local[0].shape, local[3].shape[1]):
            return on_device_fused(*local)
        return on_device_windows(*local)

    return jax.shard_map(
        on_device, mesh=mesh, in_specs=in_specs, out_specs=out_specs, check_vma=False
    )
```

```python
import jax
import jax.numpy as jnp
from jax import lax
from jax.experimental import pallas as pl
from jax.experimental.pallas import tpu as pltpu
from jax.sharding import PartitionSpec as P

HD = 128
GROUP = 2048


def passed_along(value, axis, by):
    peers = lax.axis_size(axis)
    return lax.ppermute(value, axis, [(i, (i + by) % peers) for i in range(peers)])


def placed_visible(row_count, window_rows, seq_total, first_row, back_rows, roll_by):
    query_pos = first_row + lax.broadcasted_iota(jnp.int32, (row_count, window_rows), 0)
    key_pos = (
        first_row
        - back_rows
        + seq_total
        + lax.broadcasted_iota(jnp.int32, (row_count, window_rows), 1)
    ) % seq_total
    query_order = (query_pos - roll_by + seq_total) % seq_total
    key_order = (key_pos - roll_by + seq_total) % seq_total
    return (query_order // GROUP == key_order // GROUP) & (key_order <= query_order)


def softmax_rows(query_head, keys_head, visible):
    scores = lax.dot_general(
        query_head, keys_head, (((1,), (1,)), ((), ())), preferred_element_type=jnp.float32
    )
    scores = jnp.where(visible, scores * HD ** (-0.5), -jnp.inf)
    highest = jnp.max(scores, axis=1, keepdims=True)
    powers = jnp.exp(scores - highest)
    return powers / jnp.sum(powers, axis=1, keepdims=True)


def head_forward(query_head, window_head, visible):
    prob = softmax_rows(query_head, window_head[0], visible)
    return jnp.dot(
        prob.astype(jnp.bfloat16), window_head[1], preferred_element_type=jnp.float32
    ).astype(jnp.bfloat16)


def head_backward(query_head, window_head, dout_head, visible):
    prob = softmax_rows(query_head, window_head[0], visible)
    prob_lo = prob.astype(jnp.bfloat16)
    dprob = lax.dot_general(
        dout_head, window_head[1], (((1,), (1,)), ((), ())), preferred_element_type=jnp.float32
    )
    delta = jnp.sum(prob * dprob, axis=1, keepdims=True)
    dscore = (prob * (dprob - delta) * HD ** (-0.5)).astype(jnp.bfloat16)
    grad_q = jnp.dot(dscore, window_head[0], preferred_element_type=jnp.float32).astype(
        jnp.bfloat16
    )
    grad_k = lax.dot_general(
        dscore, query_head, (((0,), (0,)), ((), ())), preferred_element_type=jnp.float32
    )
    grad_v = lax.dot_general(
        prob_lo, dout_head, (((0,), (0,)), ((), ())), preferred_element_type=jnp.float32
    )
    return (grad_q, jnp.stack((grad_k.astype(jnp.bfloat16), grad_v.astype(jnp.bfloat16))))


def attend_window(query_rows, window, dout_rows, visible):
    row_count, feat_count = query_rows.shape
    heads_here = feat_count // HD
    window_rows = window.shape[1]
    window_heads = window.reshape(2, window_rows, heads_here, HD).transpose(2, 0, 1, 3)
    query_heads = query_rows.reshape(row_count, heads_here, HD).transpose(1, 0, 2)
    dout_heads = dout_rows.reshape(row_count, heads_here, HD).transpose(1, 0, 2)
    attn_heads = lax.map(
        lambda pieces: head_forward(pieces[0], pieces[1], visible), (query_heads, window_heads)
    )
    grad_q_heads, pair_heads = lax.map(
        lambda pieces: head_backward(pieces[0], pieces[1], pieces[2], visible),
        (query_heads, window_heads, dout_heads),
    )
    attention_output = attn_heads.transpose(1, 0, 2).reshape(row_count, feat_count)
    query_gradient = grad_q_heads.transpose(1, 0, 2).reshape(row_count, feat_count)
    pair_grads = pair_heads.transpose(1, 2, 0, 3).reshape(2, window_rows, feat_count)
    return (attention_output, query_gradient, pair_grads)


def on_device_windows(
    head_query_rows,
    head_key_rows,
    head_value_rows,
    output_gradient,
    output_matrix,
    adapter_down_weight,
    adapter_up_weight,
):
    tokens_dev, feat_dev = head_query_rows.shape
    head_index = lax.axis_index("head")
    shifted = head_index >= lax.axis_size("head") // 2
    total_gradient = lax.all_gather(output_gradient, "head", axis=1, tiled=True)
    projected_output = lax.dot_general(
        total_gradient,
        lax.all_gather(output_matrix, "sub", axis=1, tiled=True),
        (((1,), (1,)), ((), ())),
        preferred_element_type=jnp.float32,
    )
    adapter_upward = lax.dot_general(
        total_gradient,
        adapter_up_weight,
        (((1,), (1,)), ((), ())),
        preferred_element_type=jnp.float32,
    )
    adapter_backward = jnp.dot(
        adapter_upward, adapter_down_weight.astype(jnp.float32).T, precision=lax.Precision.HIGHEST
    )
    attention_gradient = (projected_output + 2.0 * adapter_backward).astype(jnp.bfloat16)
    sub_count = lax.axis_size("sub")
    block_rows = tokens_dev * sub_count
    seq_total = block_rows * lax.axis_size("seq")
    reach = max(GROUP // block_rows - 1, 1)
    roll_by = jnp.where(shifted, GROUP // 2, 0)
    stacked = jnp.stack((head_query_rows, head_key_rows, head_value_rows, attention_gradient))
    moved = lax.all_to_all(stacked, "sub", split_axis=2, concat_axis=1, tiled=True)
    own_pair = moved[1:3]
    received = [passed_along(own_pair, "seq", distance) for distance in range(reach, 0, -1)]
    window = jnp.concatenate(received + [own_pair], axis=1)
    first_row = lax.axis_index("seq") * block_rows
    visible = placed_visible(
        block_rows, window.shape[1], seq_total, first_row, reach * block_rows, roll_by
    )
    attn_local, grad_q_local, pair_grads = attend_window(moved[0], window, moved[3], visible)
    running = pair_grads[:, reach * block_rows :].astype(jnp.float32)
    for distance in range(1, reach + 1):
        begin_row = (reach - distance) * block_rows
        block_terms = pair_grads[:, begin_row : begin_row + block_rows]
        returned = passed_along(block_terms, "seq", -distance)
        running = running + returned.astype(jnp.float32)
    pair_local = running.astype(jnp.bfloat16)
    back = jnp.stack((attn_local, grad_q_local, pair_local[0], pair_local[1]))
    restored = lax.all_to_all(back, "sub", split_axis=1, concat_axis=2, tiled=True)
    attention_output = restored[0]
    query_gradient = restored[1]
    key_gradient = restored[2]
    value_gradient = restored[3]
    middle_piece = jnp.dot(
        attention_output, adapter_down_weight, preferred_element_type=jnp.float32
    )
    down_gradient_part = 2.0 * jnp.dot(
        attention_output.astype(jnp.float32).T, adapter_upward, precision=lax.Precision.HIGHEST
    )
    adapter_middle = lax.psum(middle_piece, "head")
    up_gradient_part = 2.0 * jnp.dot(
        adapter_middle.T, output_gradient.astype(jnp.float32), precision=lax.Precision.HIGHEST
    )
    adapter_down_gradient, adapter_up_gradient = lax.psum(
        (down_gradient_part, up_gradient_part), ("seq", "sub")
    )
    return (
        query_gradient,
        key_gradient,
        value_gradient,
        adapter_down_gradient,
        adapter_up_gradient,
    )


SCALE = HD ** (-0.5)
F32, BF16 = jnp.float32, jnp.bfloat16


def dot_nn(left, right):
    return lax.dot_general(left, right, (((1,), (0,)), ((), ())), preferred_element_type=F32)


def dot_nt(left, right):
    return lax.dot_general(left, right, (((1,), (1,)), ((), ())), preferred_element_type=F32)


MESH = pl.DeviceIdType.MESH
BLOCKS = 4
CUTS = 2
PIECES = 1
LOG2E = 1.4426950408889634
NONE = -1e30


NAMES = (
    "big0", "big1", "kv", "q", "kvx", "qx", "kvp", "kvxp", "g", "gx", "w", "a", "b", "gl", "part0",
    "part1", "lora0", "lora1", "up", "stat", "share", "theirs0", "theirs1", "theirs2", "home",
    "home2", "far", "far2", "mid", "midx", "us", "uy", "ur", "uh", "ds", "dn",
)
PLACES = {name: place for place, name in enumerate(NAMES)}
GROUPS = 8
TALLY, BLOCK_BYTES = 1024, 4096


def combine(mine, other):
    top = jnp.maximum(mine[0], other[0])
    c = SCALE * LOG2E
    e1, e2 = jnp.exp2((mine[0] - top) * c), jnp.exp2((other[0] - top) * c)
    w = 1.0 / (mine[1] * e1 + other[1] * e2)
    return e1 * w, e2 * w


def fused_kernel(
    q_ref, k_ref, v_ref, g_ref, w_ref, a_hbm, b_hbm,
    dq_out, dk_out, dv_out, down_out, up_out,
    qb, kb, vb, gb, qr, kr, vr, gr,
    a_ref, b_ref, big, wb, gl, xb, xs, xr, ls, lr, lt, lub, dob,
    kt, vt, probs, ot, gt, acc, stat_s, stat_r, share_s, share_r, ts, tr, hs, dqs,
    rk, rv, rq, ms, mb, mf, mxs, mxr, us, usr, ys, yr, zo, uf, dss, dsr, dnr,
    tally, ssem, rsem,
):
    s, x, c = lax.axis_index("seq"), lax.axis_index("head"), lax.axis_index("sub")
    n = BLOCKS
    half, j = s // n, lax.rem(s, n)
    late = lax.rem(half + x, 2) == 1
    early = lax.rem(half + x, 2) == 0
    partner = {"sub": 1 - c}
    p = PLACES
    held = {"always": None, "late": late, "early": early, "other": c != x}
    groups = []

    def at(base, many):
        return pl.ds(pl.multiple_of(base, many), many)

    def send(src, dst, place, to, when="always"):
        size = src.dtype.itemsize
        for extent in src.shape:
            size *= extent
        for group in groups:
            if group[0] == when and group[1] + size <= TALLY * BLOCK_BYTES:
                break
        else:
            group = [when, 0]
            groups.append(group)
        group[1] += size
        copy = pltpu.make_async_remote_copy(
            src_ref=src, dst_ref=dst, send_sem=ssem.at[groups.index(group)], recv_sem=rsem.at[p[place]],
            device_id=to, device_id_type=MESH,
        )
        if held[when] is None:
            copy.start()
        else:
            pl.when(held[when])(copy.start)

    def all_sent():
        for i, (when, size) in enumerate(groups):
            sent = tally.at[pl.ds(0, size // BLOCK_BYTES)]
            copy = pltpu.make_async_remote_copy(
                src_ref=sent, dst_ref=sent, send_sem=ssem.at[i], recv_sem=rsem.at[0],
                device_id=partner, device_id_type=MESH,
            )
            if held[when] is None:
                copy.wait_send()
            else:
                pl.when(held[when])(copy.wait_send)

    def got(ref, place):
        pltpu.make_async_remote_copy(
            src_ref=ref, dst_ref=ref, send_sem=ssem.at[0], recv_sem=rsem.at[p[place]],
            device_id=partner, device_id_type=MESH,
        ).wait_recv()

    def local(src, dst, place):
        copy = pltpu.make_async_copy(src, dst, rsem.at[p[place]])
        copy.start()
        return copy

    def near(d):
        o = lax.rem(j + d, n)
        return o, {"seq": half * n + o}

    def far(d):
        o = lax.rem(j + d, n)
        return o, {"seq": (1 - half) * n + o}

    barrier = pltpu.get_barrier_semaphore()
    greeted = [near(d)[1] for d in range(1, n)] + [far(d)[1] for d in range(n)]
    pair_s = s + 1 - 2 * lax.rem(s, 2)
    greeted += [{"seq": pair_s, "sub": 1 - c}, partner, {"head": 1 - x}, {"head": 1 - x, "sub": 1 - c}]
    for device in greeted:
        pl.semaphore_signal(barrier, inc=1, device_id=device, device_id_type=MESH)
    pl.semaphore_wait(barrier, len(greeted))

    part_rows = HD // CUTS
    for r in range(CUTS):
        mine_g = at(r * 2 * part_rows + c * part_rows, part_rows)
        from_g = g_ref.at[pl.ds(r * part_rows, part_rows)]
        place = f"big{r}"
        send(from_g, big.at[mine_g], place, {"head": 1 - x, "sub": x})
        send(from_g, big.at[mine_g], place, partner, when="other")

        @pl.when(c == x)
        def _():
            local(from_g, big.at[mine_g], place)

    w_copy = local(w_ref, wb, "w")
    low_rank_copies = [local(a_hbm, a_ref, "a"), local(b_hbm, b_ref, "b")]
    mine_k, mine_q = at(j * 2 * HD + c * HD, HD), at(j * HD, HD)
    own = at(j * 2 * HD, 2 * HD)
    for d in range(1, n):
        o, to = near(d)
        cols = at(o * 2 * HD, 2 * HD)
        send(k_ref.at[:, cols], kb.at[mine_k], "kv", to)
        send(v_ref.at[:, cols], vb.at[mine_k], "kv", to)
        send(q_ref.at[:, cols], qb.at[mine_q], "q", to)
    for d in range(n):
        o, to = far(d)
        first, second = at(o * 2 * HD, HD), at(o * 2 * HD + HD, HD)
        send(k_ref.at[:, first], kr.at[mine_k], "kvx", to, when="early")
        send(v_ref.at[:, first], vr.at[mine_k], "kvx", to, when="early")
        send(q_ref.at[:, second], qr.at[mine_q], "qx", to, when="late")
    local(k_ref.at[:, own], kb.at[mine_k], "kv")
    local(v_ref.at[:, own], vb.at[mine_k], "kv")
    local(q_ref.at[:, own], qb.at[mine_q], "q")
    send(k_ref.at[:, own], kb.at[mine_k], "kvp", partner)
    send(v_ref.at[:, own], vb.at[mine_k], "kvp", partner)
    gl_copy = local(g_ref, gl, "gl")

    w_copy.wait()
    for copy in low_rank_copies:
        copy.wait()
    feats, cols_dev, width = wb.shape[0], big.shape[1], 2 * HD
    ups = []

    def project_cut(r):
        both = pl.ds(r * 2 * part_rows, 2 * part_rows)
        got(big.at[both], f"big{r}")

        def project(f, carry):
            piece = at(f * width, width)
            xb[both, piece] = dot_nt(big[both, :], wb[piece, :])
            return carry

        ls[r] = dot_nt(b_ref[:, at(c * cols_dev, cols_dev)], big[both, :])
        send(ls.at[r], lr.at[r], f"lora{r}", partner)
        lax.fori_loop(0, feats // width, project, 0)
        span = pl.ds(r * part_rows, part_rows)
        xs[span, :] = xb[at((2 * r + 1 - c) * part_rows, part_rows), :].astype(BF16)
        send(xs.at[span], xr.at[span], f"part{r}", partner)

    def gradient_cut(r):
        span = pl.ds(r * part_rows, part_rows)
        got(lr.at[r], f"lora{r}")
        up_r = ls[r] + lr[r]
        lt[...] = (2.0 * up_r).T
        ups.append(up_r)
        lora = dot_nn(lt[at(c * part_rows, part_rows), :].astype(BF16), a_ref[...])
        got(xr.at[span], f"part{r}")
        own_x = xb[at((2 * r + c) * part_rows, part_rows), :]
        dob[span, :] = (own_x + xr[span, :].astype(F32) + lora).astype(BF16)
        mine_d = at(j * HD + r * part_rows, part_rows)
        for d in range(1, n):
            o, to = near(d)
            send(dob.at[span, at(o * 2 * HD, 2 * HD)], gb.at[mine_d], "g", to)
        for d in range(n):
            o, to = far(d)
            send(dob.at[span, at(o * 2 * HD + HD, HD)], gr.at[mine_d], "gx", to, when="late")

    for r in range(CUTS - 1):
        project_cut(r)
        gradient_cut(r)
    project_cut(CUTS - 1)
    got(kb, "kv")
    for d in range(1, n):
        o = lax.rem(j + d, n)
        block = at(o * 2 * HD + c * HD, HD)
        send(kb.at[block], kb.at[block], "kvp", partner)
        send(vb.at[block], vb.at[block], "kvp", partner)

    gradient_cut(CUTS - 1)
    gb[mine_q, :] = dob[:, own]
    up_mine = jnp.where(
        c == 0,
        jnp.concatenate([u[:, :part_rows] for u in ups], axis=1),
        jnp.concatenate([u[:, part_rows:] for u in ups], axis=1),
    )
    here = lub.at[half, :, at(j * HD, HD)]
    lub[half, :, at(j * HD, HD)] = up_mine.astype(BF16)
    for d in range(1, n):
        o, to = near(d)
        send(here, here, "up", to)
    for d in range(n):
        o, to = far(d)
        send(here, here, "up", to)

    @pl.when(late)
    def _():
        got(kr, "kvx")

    for o in range(n):
        block = at(o * 2 * HD + c * HD, HD)
        send(kr.at[block], kr.at[block], "kvxp", partner, when="late")
        send(vr.at[block], vr.at[block], "kvxp", partner, when="late")
    got(qb, "q")
    got(kb, "kvp")

    @pl.when(late)
    def _():
        got(kr, "kvxp")
        qr[...] = qb[:, :HD]

    @pl.when(early)
    def _():
        got(qr, "qx")
        kr[...] = kb[:, HD:]
        vr[...] = vb[:, HD:]

    tile = 2 * HD
    total = kb.shape[0]
    lanes = (slice(0, HD), slice(HD, 2 * HD), slice(0, HD))
    keys, values = (kb, kb, kr), (vb, vb, vr)
    queries, douts = (qb, qb, qr), (gb, gb, gr)
    key_at = lax.broadcasted_iota(jnp.int32, (2 * tile, tile), 0)
    row = lax.broadcasted_iota(jnp.int32, (2 * tile, tile), 1)
    seen = key_at <= row + jnp.where(row >= HD, HD, 0) + c * HD

    def extent(part, u):
        return total if part == 2 else (u + 1) * 2 * tile

    tops, sums = [], []
    for part in range(3):
        kt[part] = keys[part][:, lanes[part]].T
        vt[part] = values[part][:, lanes[part]].T
        queries_t = queries[part][:, lanes[part]].T
        top_u, sum_u = [], []
        for u in range(2):
            ext = extent(part, u)
            q_t = queries_t[:, u * tile : (u + 1) * tile]
            scores = dot_nn(keys[part][:ext, lanes[part]], q_t)
            if part < 2:
                settled = ext - 2 * tile
                edge = jnp.where(seen, scores[settled:, :], NONE)
                scores = edge if settled == 0 else jnp.concatenate((scores[:settled, :], edge), axis=0)
            top = jnp.max(scores, axis=0, keepdims=True)
            powers = jnp.exp2((scores - top) * (SCALE * LOG2E))
            top_u.append(top)
            sum_u.append(jnp.sum(powers, axis=0, keepdims=True))
            low = powers.astype(BF16)
            probs[part, :ext, u * tile : (u + 1) * tile] = low
            ot[part, :, u * tile : (u + 1) * tile] = dot_nn(vt[part, :, :ext], low)
        tops.append(jnp.concatenate(top_u, axis=1))
        sums.append(jnp.concatenate(sum_u, axis=1))

    local_stats = [(tops[part], sums[part]) for part in range(3)]
    for r in range(2):
        stat_s[r : r + 1, :] = jnp.where(late, local_stats[1][r], local_stats[2][r])
    nothing = (NONE, 0.0)
    other_0 = tuple(jnp.where(late, local_stats[2][r], nothing[r]) for r in range(2))
    first, second = combine(local_stats[0], other_0)
    attn_0 = (ot[0] * first + jnp.where(late, ot[2] * second, 0.0)).astype(BF16)
    down = [a_ref[:, at(j * 2 * HD + i * HD, HD)] for i in range(2)]
    alone = ot[1] * jnp.where(late, 1.0, 1.0 / sums[1])
    mid_0, mid_1 = dot_nn(down[0], attn_0), dot_nn(down[1], alone.astype(BF16))
    rank = mid_0.shape[0]
    ms[:rank, :] = mid_0 + jnp.where(late, 0.0, mid_1)
    ms[rank : 2 * rank, :] = jnp.where(late, mid_1, dot_nn(down[1], ot[2].astype(BF16)))
    ms[2 * rank :, :] = stat_s[...]
    for d in range(1, n):
        o, to = near(d)
        send(ms.at[:, at(o * HD, HD)], mb.at[j], "mid", to, when="late")
        send(ms.at[pl.ds(0, rank), at(o * HD, HD)], mb.at[j, pl.ds(0, rank)], "mid", to, when="early")
    for d in range(n):
        o, to = far(d)
        send(ms.at[pl.ds(rank, rank + 8), at(o * HD, HD)], mf.at[j], "far", to, when="early")
    mb[j] = ms[:, at(j * HD, HD)]
    send(stat_s, stat_r, "stat", {"seq": (1 - half) * n + j})

    def backward(part, w, delta):
        delta = delta * w
        for u in reversed(range(2)):
            ext = extent(part, u)
            span = slice(u * tile, (u + 1) * tile)
            g_t = gt[part, :, span] * w[:, span]
            g = g_t.T.astype(BF16)
            low = probs[part, :ext, span]
            dprob = dot_nn(values[part][:ext, lanes[part]], g_t.astype(BF16))
            dscore = (dprob - delta[:, span]).astype(BF16) * low
            dq_t = dot_nn(kt[part, :, :ext], dscore)
            dq = (dq_t * SCALE).T
            dk = dot_nn(dscore, queries[part][span, lanes[part]])
            dv = dot_nn(low, g)
            at_k, at_v = 2 * part, 2 * part + 1
            if u == 1:
                acc[at_k], acc[at_v] = dk, dv
            else:
                acc[at_k, :ext, :] += dk
                acc[at_v, :ext, :] += dv
            dqs[part, span, :] = dq

    def to_partner(part, when="always"):
        for t, scale in ((2 * part, SCALE), (2 * part + 1, 1.0)):
            for o in range(n):
                block = acc[t, at(o * 2 * HD + (1 - c) * HD, HD), :]
                ts[t, pl.ds(o * HD, HD), :] = (block * scale).astype(BF16)
        both = pl.ds(2 * part, 2)
        send(ts.at[both], tr.at[both], f"theirs{part}", partner, when=when)

    def add_theirs(part):
        got(tr.at[pl.ds(2 * part, 2)], f"theirs{part}")
        for t, scale in ((2 * part, SCALE), (2 * part + 1, 1.0)):
            for o in range(n):
                span = pl.ds(o * HD, HD)
                block = acc[t, at(o * 2 * HD + c * HD, HD), :]
                hs[t, span, :] = (block * scale + tr[t, span, :].astype(F32)).astype(BF16)

    def home_sends(part, t, out):
        cols = at(j * 2 * HD + part * HD, HD)
        for d in range(1, n):
            o, to = near(d)
            send(hs.at[t, at(o * HD, HD)], out.at[:, cols], "home", to)
        out[:, cols] = hs[t, mine_q, :]

    def pair_home(part):
        add_theirs(part)
        home_sends(part, 2 * part, dk_out)
        home_sends(part, 2 * part + 1, dv_out)

    got(gb.at[pl.ds(0, (n - 1) * HD)], "g")

    @pl.when(late)
    def _():
        gr[...] = gb[:, :HD]

    @pl.when(early)
    def _():
        got(gr, "gx")

    shares = []
    for part in range(3):
        g_t = douts[part][:, lanes[part]].astype(F32).T
        gt[part] = g_t
        shares.append(jnp.sum(ot[part] * g_t, axis=0, keepdims=True))
    share_s[...] = jnp.broadcast_to(jnp.where(late, shares[1], shares[2]), share_s.shape)
    send(share_s, share_r, "share", {"seq": (1 - half) * n + j})
    backward(0, first, first * shares[0] + second * jnp.where(late, shares[2], 0.0))
    to_partner(0)

    @pl.when(late)
    def _():
        got(mb.at[pl.ds(0, n - 1)], "mid")

    @pl.when(early)
    def _():
        got(mb.at[pl.ds(0, n - 1), pl.ds(0, rank)], "mid")

    mid = mb[0, :rank, :]
    for o in range(1, n):
        mid = mid + mb[o, :rank, :]
    mxs[...] = mid

    @pl.when(late)
    def _():
        got(mf, "far")
        whole = mxs[...]
        for o in range(n):
            near_stat = (mb[o, 2 * rank : 2 * rank + 1, :], mb[o, 2 * rank + 1 : 2 * rank + 2, :])
            far_stat = (mf[o, rank : rank + 1, :], mf[o, rank + 1 : rank + 2, :])
            w_near, w_far = combine(near_stat, far_stat)
            whole = whole + mb[o, rank : 2 * rank, :] * w_near + mf[o, :rank, :] * w_far
        mxs[...] = whole

    send(mxs, mxr, "midx", {"head": 1 - x})
    pair_home(0)
    gl_copy.wait()
    got(mxr, "midx")
    mid = (2.0 * (mxs[...] + mxr[...])).astype(BF16)
    up = dot_nn(mid, gl[...])
    side = us.shape[2]
    us[0], us[1] = up[:, :side], up[:, side:]
    send(us.at[1 - c], usr, "us", partner)
    got(stat_r, "stat")
    remote = (stat_r[0:1, :], stat_r[1:2, :])
    other_1 = tuple(jnp.where(late, remote[r], nothing[r]) for r in range(2))
    other_2 = tuple(jnp.where(late, local_stats[0][r], remote[r]) for r in range(2))
    w_1, w_2 = combine(local_stats[1], other_1), combine(local_stats[2], other_2)
    attn_1 = (ot[1] * w_1[0]).astype(BF16)
    attn_2 = (ot[2] * w_2[0]).astype(BF16)
    got(b_ref.at[:, pl.ds(0, (2 * n - 1) * HD)], "up")
    near_up = lub[half]
    dss[:, :HD] = dot_nt(near_up, attn_0)
    dss[:, HD:] = dot_nt(near_up, attn_1) + jnp.where(late, 0.0, dot_nt(lub[1 - half], attn_2))
    send(dss, dsr, "ds", partner)
    got(usr, "us")
    us[c] += usr[...]
    quarter, mine_y = side // 2, lax.rem(s, 2)
    ys[...] = us[c, :, at((1 - mine_y) * quarter, quarter)].astype(BF16)
    send(ys, yr, "uy", {"seq": pair_s})
    got(share_r, "share")
    far_share = share_r[0:1, :]
    backward(2, w_2[0], w_2[0] * shares[2] + w_2[1] * jnp.where(late, shares[0], far_share))
    got(dsr, "ds")
    dnr[s] = (2.0 * (dss[...] + dsr[...])).astype(BF16)
    for d in range(1, 2 * n):
        other = lax.rem(s + d, 2 * n)
        send(dnr.at[s], dnr.at[s], "dn", {"seq": other})
    to_partner(2, when="late")
    hs[6] = (dqs[0] + jnp.where(late, dqs[2], 0.0)).astype(BF16)
    home_sends(0, 6, dq_out)

    @pl.when(early)
    def _():
        hs[8] = dqs[2].astype(BF16)

    for d in range(n):
        o, to = far(d)
        send(hs.at[8, at(o * HD, HD)], rq.at[j], "far2", to, when="early")
    backward(1, w_1[0], w_1[0] * shares[1] + w_1[1] * jnp.where(late, far_share, 0.0))
    for t in (0, 1):
        acc[2 + t] += jnp.where(early, acc[4 + t], 0.0)
    to_partner(1)
    hs[7] = dqs[1].astype(BF16)
    home_sends(1, 7, dq_out)
    got(yr, "uy")
    level = s // 2
    zo[level] = (us[c, :, at(mine_y * quarter, quarter)] + yr[...].astype(F32)).astype(BF16)
    for d in range(1, n):
        send(zo.at[level], zo.at[level], "ur", {"seq": lax.rem(s + 2 * d, 2 * n)})

    @pl.when(late)
    def _():
        add_theirs(2)

    for t, to_ref in ((4, rk), (5, rv)):
        for d in range(n):
            o, to = far(d)
            send(hs.at[t, at(o * HD, HD)], to_ref.at[j], "home2", to, when="late")
    pair_home(1)
    got(dnr.at[pl.ds(0, 2 * n - 1)], "dn")
    for i in range(n):
        down_out[:, i * 2 * HD : (i + 1) * 2 * HD] = dnr[i].astype(F32) + dnr[i + n].astype(F32)
    got(zo.at[pl.ds(0, n - 1)], "ur")
    total_up = zo[0].astype(F32)
    for i in range(1, n):
        total_up = total_up + zo[i].astype(F32)
    mine = at(c * side + mine_y * quarter, quarter)
    uf[:, mine] = total_up
    for to in ({"seq": pair_s}, partner, {"seq": pair_s, "sub": 1 - c}):
        send(uf.at[:, mine], uf.at[:, mine], "uh", to)

    blocks = 6 * (n - 1) * HD * HD // probs.shape[2]
    got(probs.at[0, pl.ds(0, blocks)], "home")

    @pl.when(late)
    def _():
        got(rq, "far2")
        for o in range(n):
            cols = slice(o * 2 * HD + HD, (o + 1) * 2 * HD)
            dq_out[:, cols] = (dq_out[:, cols].astype(F32) + rq[o].astype(F32)).astype(BF16)

    @pl.when(early)
    def _():
        got(kr, "home2")
        for out, ref in ((dk_out, rk), (dv_out, rv)):
            for o in range(n):
                cols = slice(o * 2 * HD, o * 2 * HD + HD)
                out[:, cols] = (out[:, cols].astype(F32) + ref[o].astype(F32)).astype(BF16)

    got(uf.at[:, pl.ds(0, 3 * quarter)], "uh")
    up_out[...] = uf[...]
    all_sent()


def written(*arrays):
    def kernel(*refs):
        copies = []
        for i, array in enumerate(arrays):
            rows = array.shape[0] // PIECES
            for k in range(PIECES):
                piece = pl.ds(k * rows, rows)
                copies.append(
                    pltpu.make_async_copy(
                        refs[i].at[piece], refs[len(arrays) + i].at[piece], refs[-1].at[i, k]
                    )
                )
        for copy in copies:
            copy.start()
        for copy in copies:
            copy.wait()

    return pl.pallas_call(
        kernel,
        out_shape=tuple(jax.ShapeDtypeStruct(array.shape, array.dtype) for array in arrays),
        in_specs=[pl.BlockSpec(memory_space=pltpu.VMEM)] * len(arrays),
        out_specs=[pl.BlockSpec(memory_space=pl.ANY)] * len(arrays),
        scratch_shapes=[pltpu.SemaphoreType.DMA((len(arrays), PIECES))],
    )(*arrays)


def on_device_fused(q, k, v, g, w, a, b):
    rows, feats = q.shape
    cols = g.shape[1]
    rank = b.shape[0]
    tokens, window = BLOCKS * rows, 2 * BLOCKS * rows
    vmem, hbm = pl.BlockSpec(memory_space=pltpu.VMEM), pl.BlockSpec(memory_space=pl.ANY)
    scratch = [
        ((tokens, 2 * HD), BF16), ((window, 2 * HD), BF16), ((window, 2 * HD), BF16), ((tokens, 2 * HD), BF16),
        ((tokens, HD), BF16), ((window, HD), BF16), ((window, HD), BF16), ((tokens, HD), BF16),
        ((rank, feats), BF16), (b.shape, BF16), ((2 * rows, cols), BF16), (w.shape, BF16), ((rows, cols), BF16), ((2 * rows, feats), F32),
        ((rows, feats), BF16), ((rows, feats), BF16), ((CUTS, rank, 2 * rows // CUTS), F32), ((CUTS, rank, 2 * rows // CUTS), F32),
        ((2 * rows // CUTS, rank), F32), ((2, rank, tokens), BF16), ((rows, feats), BF16),
        ((3, HD, window), BF16), ((3, HD, window), BF16), ((3, window, tokens), BF16), ((3, HD, tokens), F32),
        ((3, HD, tokens), F32), ((6, window, HD), F32), ((8, tokens), F32), ((8, tokens), F32), ((8, tokens), F32), ((8, tokens), F32),
        ((6, tokens, HD), BF16), ((6, tokens, HD), BF16), ((9, tokens, HD), BF16), ((3, tokens, HD), F32),
        ((BLOCKS, rows, HD), BF16), ((BLOCKS, rows, HD), BF16), ((BLOCKS, rows, HD), BF16),
        ((2 * rank + 8, tokens), F32), ((BLOCKS, 2 * rank + 8, rows), F32), ((BLOCKS, rank + 8, rows), F32), ((rank, rows), F32), ((rank, rows), F32),
        ((2, rank, cols // 2), F32), ((rank, cols // 2), F32), ((rank, cols // 4), BF16), ((rank, cols // 4), BF16),
        ((BLOCKS, rank, cols // 4), BF16), ((rank, cols), F32), ((rank, 2 * HD), F32), ((rank, 2 * HD), F32), ((2 * BLOCKS, rank, 2 * HD), BF16),
        ((TALLY, 8, HD), F32),
    ]
    dq, dk, dv, down, up = pl.pallas_call(
        fused_kernel,
        out_shape=(
            jax.ShapeDtypeStruct((rows, feats), BF16),
            jax.ShapeDtypeStruct((rows, feats), BF16),
            jax.ShapeDtypeStruct((rows, feats), BF16),
            jax.ShapeDtypeStruct((rank, feats), F32),
            jax.ShapeDtypeStruct((rank, cols), F32),
        ),
        in_specs=[hbm] * 7,
        out_specs=[vmem] * 5,
        scratch_shapes=[pltpu.VMEM(shape, kind) for shape, kind in scratch]
        + [pltpu.SemaphoreType.DMA((GROUPS,)), pltpu.SemaphoreType.DMA((len(PLACES),))],
        compiler_params=pltpu.CompilerParams(
            collective_id=0, has_side_effects=True, vmem_limit_bytes=60 * 1024 * 1024
        ),
    )(q, k, v, g, w, a.T, b)
    dq, dk, dv, down, up = written(dq, dk, dv, down, up)
    return dq, dk, dv, down.T, up


def one_group(mesh, rows, feats, width):
    seq, head, sub = mesh.shape["seq"], mesh.shape["head"], mesh.shape["sub"]
    return (
        sub == 2
        and head == 2
        and rows == HD
        and seq == 2 * BLOCKS
        and seq * sub * rows == GROUP
        and feats == seq * HD
        and width == 2 * seq * HD
    )


def solution(mesh):
    in_specs = (
        P(("rep", "seq", "sub"), "head"),
        P(("rep", "seq", "sub"), "head"),
        P(("rep", "seq", "sub"), "head"),
        P(("rep", "seq", "sub"), "head"),
        P("head", "sub"),
        P("head", None),
        P(),
    )
    out_specs = (
        P(("rep", "seq", "sub"), "head"),
        P(("rep", "seq", "sub"), "head"),
        P(("rep", "seq", "sub"), "head"),
        P(("rep", "head"), None),
        P("rep", "head"),
    )

    def on_device(*local):
        if one_group(mesh, *local[0].shape, local[3].shape[1]):
            return on_device_fused(*local)
        return on_device_windows(*local)

    return jax.shard_map(
        on_device, mesh=mesh, in_specs=in_specs, out_specs=out_specs, check_vma=False
    )
```
